32 devices in a mesh: gx: 4 (over y, x), gy: 4 (over z), gz: 2 (over core).
Axes of the slice: x: 2, y: 2, z: 4, core: 2. Of those that a mesh axis runs over, the one named last changes fastest.
Arguments:
- coarse: bfloat16 [2, 5, 8, 32, 128], P(None, None, 'gz', 'gx', 'gy'), may hold values from -1.5 to 1.5
- detail_x1: bfloat16 [2, 5, 8, 32, 128], P(None, None, 'gz', 'gx', 'gy'), may hold values from -1 to 1
- detail_y1: bfloat16 [2, 5, 8, 64, 128], P(None, None, 'gz', 'gx', 'gy'), may hold values from -1 to 1
- detail_x2: bfloat16 [2, 5, 8, 64, 256], P(None, None, 'gz', 'gx', 'gy'), may hold values from -1 to 1
- detail_y2: bfloat16 [2, 5, 8, 128, 256], P(None, None, 'gz', 'gx', 'gy'), may hold values from -1 to 1
- significance: int32 [2, 8, 16, 16], P(None, 'gz', 'gx', 'gy'), may hold values 0 or 1
- adjoint: float32 [5, 8, 128, 512], P(None, 'gz', 'gx', 'gy'), may hold values from -6 to 6
Outputs:
- adjoint_next: float32 [5, 8, 128, 512], P(None, 'gz', 'gx', 'gy')
The draws below stay inside these ranges and needn't reach their ends.
Inputs may be any that keep to these rules, and one draw needn't show every extreme that they name: `significance`: each entry flags one tile.
All inputs are finite; a program needn't handle non-finite values. No bound on the sum of `significance` on one device may be relied on, other than what follows from the above.
Results may differ from the reference program's by a relative error of at most 0.0012.
Values may be sent and summed in bfloat16 or wider, within the bound.
A program may use at most 64 MiB of HBM per device.

```python
import jax
import jax.numpy as jnp
from jax import lax

NX = 128
NY = 512
NZ = 8


def plant(values, key, low, high):
    extent = values.shape
    place = [jax.random.randint(jax.random.fold_in(key, axis), (), 0, extent[axis]) for axis in range(len(extent))]
    values = values.at[tuple(place)].set(low)
    longest = extent.index(max(extent))
    place[longest] = (place[longest] + 1) % extent[longest]
    return values.at[tuple(place)].set(high)


def shard_levels(own_key, dims, shards, smallest, largest):
    gain, own = 1.0, jax.random.fold_in(own_key, 6)
    for position, shards_of in shards:
        heights = jnp.exp(jax.random.uniform(jax.random.fold_in(own, position), (shards_of,), jnp.float32, smallest / len(shards), largest / len(shards)))
        gain = gain * jnp.repeat(heights, dims[position] // shards_of).reshape([-1 if axis == position else 1 for axis in range(len(dims))])
    return gain


def scatter_about(stream_key, dims, deviation, reach, pieces=(), kind=jnp.bfloat16):
    values = jax.random.normal(stream_key, dims, jnp.float32) * deviation
    if len(pieces) > 0:
        values = shard_levels(stream_key, dims, pieces, -0.22, 0.18) * values
    return jnp.clip(values, min=-reach, max=reach).astype(kind)


def setup_inputs(seed: int = 0) -> dict:
    streams_of = jax.random.split(jax.random.key(seed), 8)
    return {
        "coarse": scatter_about(streams_of[0], (2, 5, NZ, NX // 4, NY // 4), 0.5, 1.5, ((2, 2), (3, 4), (4, 4))),
        "detail_x1": scatter_about(streams_of[1], (2, 5, NZ, NX // 4, NY // 4), 0.3, 1.0, ((2, 2), (3, 4), (4, 4))),
        "detail_y1": scatter_about(streams_of[2], (2, 5, NZ, NX // 2, NY // 4), 0.3, 1.0, ((2, 2), (3, 4), (4, 4))),
        "detail_x2": scatter_about(streams_of[3], (2, 5, NZ, NX // 2, NY // 2), 0.3, 1.0, ((2, 2), (3, 4), (4, 4))),
        "detail_y2": scatter_about(streams_of[4], (2, 5, NZ, NX, NY // 2), 0.3, 1.0, ((2, 2), (3, 4), (4, 4))),
        "significance": plant((jax.random.randint(streams_of[5], (2, NZ, NX // 8, NY // 32), 0, 4) < 3).astype(jnp.int32), jax.random.fold_in(streams_of[5], 1), 0, 1),
        "adjoint": scatter_about(streams_of[6], (5, NZ, NX, NY), 1.0, 6.0, ((1, 2), (2, 4), (3, 4)), jnp.float32),
    }


time_step = 0.1
viscosity = 0.2
heat_ratio_less_one = 0.4

def displace(values, axis_dim, offset, wrap):
    if wrap:
        return jnp.roll(values, offset, axis=axis_dim)
    length = values.shape[axis_dim]
    zeros_part = jnp.zeros_like(lax.slice_in_dim(values, 0, abs(offset), axis=axis_dim))
    if offset > 0:
        return jnp.concatenate([zeros_part, lax.slice_in_dim(values, 0, length - offset, axis=axis_dim)], axis=axis_dim)
    return jnp.concatenate([lax.slice_in_dim(values, -offset, length, axis=axis_dim), zeros_part], axis=axis_dim)

def refine(coarse_part, detail, axis_dim):
    centre = coarse_part
    behind = displace(coarse_part, axis_dim, 1, True)
    ahead_one = displace(coarse_part, axis_dim, -1, True)
    ahead_two = displace(coarse_part, axis_dim, -2, True)
    odd_values = detail + (9.0 * (centre + ahead_one) - (behind + ahead_two)) / 16.0
    stacked = jnp.stack([centre, odd_values], axis=axis_dim + 1)
    target = list(coarse_part.shape)
    target[axis_dim] = 2 * coarse_part.shape[axis_dim]
    return stacked.reshape(target)

def spread_mask(tile_flags, rows_tile, cols_tile):
    ones_block = jnp.ones((1, 1, 1, rows_tile, 1, cols_tile), jnp.float32)
    widened = tile_flags.astype(jnp.float32)[:, :, :, None, :, None] * ones_block
    return widened.reshape(tile_flags.shape[0], tile_flags.shape[1], tile_flags.shape[2] * rows_tile, tile_flags.shape[3] * cols_tile)[:, None]

def face_flux(physical_variable_set, component):
    volumetric_matter = jnp.exp(0.5 * physical_variable_set[0])
    velocity = physical_variable_set[1:4]
    thermal_state_value = physical_variable_set[4]
    thermo_normal_stress = volumetric_matter * thermal_state_value
    normal_speed = velocity[component]
    velocity_norm_square = velocity[0] * velocity[0] + velocity[1] * velocity[1] + velocity[2] * velocity[2]
    whole_conserved_work = volumetric_matter * (thermal_state_value / heat_ratio_less_one + 0.5 * velocity_norm_square)
    mass_flux = volumetric_matter * normal_speed
    momenta = [mass_flux * velocity[which] for which in range(3)]
    momenta[component] = momenta[component] + thermo_normal_stress
    return jnp.stack([mass_flux] + momenta + [normal_speed * (whole_conserved_work + thermo_normal_stress)])

def face_term(upper_state, lower_state, upper_adjoint, lower_adjoint, component):
    middle_state = 0.5 * (upper_state + lower_state)
    jump = upper_adjoint - lower_adjoint
    unused, pullback = jax.vjp(lambda values: face_flux(values, component), middle_state)
    return pullback(jump)[0]

def synthesize(coarse, detail_x1, detail_y1, detail_x2, detail_y2, significance):
    refined = refine(coarse.astype(jnp.float32), detail_x1.astype(jnp.float32), 3)
    refined = refine(refined, detail_y1.astype(jnp.float32), 4)
    refined = refine(refined, detail_x2.astype(jnp.float32) * spread_mask(significance, 4, 16), 3)
    return refine(refined, detail_y2.astype(jnp.float32) * spread_mask(significance, 8, 16), 4)

def adjoint_rate(physical_variable_set, adjoint_now):
    totals = jnp.zeros_like(adjoint_now)
    for component, axis_dim, wrap in ((0, 2, True), (1, 3, True), (2, 1, False)):
        upper_adjoint = displace(adjoint_now, axis_dim, -1, wrap)
        lower_adjoint = displace(adjoint_now, axis_dim, 1, wrap)
        face_terms = face_term(displace(physical_variable_set, axis_dim, -1, wrap), physical_variable_set, upper_adjoint, adjoint_now, component)
        totals = totals + 0.5 * face_terms + 0.5 * displace(face_terms, axis_dim, 1, wrap)
        totals = totals + viscosity * (upper_adjoint + lower_adjoint - 2.0 * adjoint_now)
    return totals

def reference(coarse, detail_x1, detail_y1, detail_x2, detail_y2, significance, adjoint):
    primitives = synthesize(coarse, detail_x1, detail_y1, detail_x2, detail_y2, significance)
    first_rate = adjoint_rate(primitives[0], adjoint)
    middle = adjoint + time_step * first_rate
    second_rate = adjoint_rate(primitives[1], middle)
    return adjoint + 0.5 * time_step * (first_rate + second_rate)
```

```python
import functools

import jax
import jax.numpy as jnp
import ml_dtypes
import numpy as np
from jax import lax
from jax.experimental import pallas as pl
from jax.experimental.pallas import tpu as pltpu
from jax.sharding import PartitionSpec as P

time_step = 0.1
viscosity = 0.2
heat_ratio_less_one = 0.4
f32 = jnp.float32
bf16 = jnp.bfloat16
MESH = pl.DeviceIdType.MESH
segments = ((0, 320, 32), (320, 640, 32), (640, 1280, 32), (1280, 1920, 64), (1920, 3200, 64))


def predict(index):
    k = index // 2
    if index % 2 == 0:
        return {("c", k): 1.0}
    return {
        ("d", k): 1.0,
        ("c", k): 9 / 16,
        ("c", k + 1): 9 / 16,
        ("c", k - 1): -1 / 16,
        ("c", k + 2): -1 / 16,
    }


def predict_twice(index):
    whole = {}
    for (kind, k), weight in predict(index).items():
        if kind == "d":
            whole[("e", k)] = weight
            continue
        whole[("m", k)] = weight
        for key, inner in predict(k).items():
            whole[key] = whole.get(key, 0.0) + weight * inner
    return whole


def lane_of(k, length):
    if k < 0:
        return 69 + k
    return k if k < length else 64 + k - length


def y_matrices():
    mats = np.zeros((4, 128, 256), np.float32)
    columns = [(y, y) for y in range(128)] + [(128, 128), (-1, 255)]
    for y, column in columns:
        for (kind, k), weight in predict_twice(y).items():
            which = "cdme".index(kind)
            mats[which, lane_of(k, 32 if which < 2 else 64), column] += weight
    return mats.astype(ml_dtypes.bfloat16)


def x_matrix():
    mat = np.zeros((48, 64), np.float32)
    for x in range(-1, 33):
        row = x + 8
        for (kind, k), weight in predict_twice(x).items():
            if kind == "c":
                at = 50 + k if k < 0 else (k if k < 8 else 56 + k - 8)
            elif kind == "d":
                at = 50 if k < 0 else (8 + k if k < 8 else 59)
            elif kind == "m":
                at = 53 + k if k < 0 else (16 + k if k < 16 else 60 + k - 16)
            else:
                at = 53 if k < 0 else 32 + k
            mat[row, at] += weight
    mat[7, 54] = 1.0
    mat[40, 62] = 1.0
    return np.concatenate([mat, mat], axis=1).astype(ml_dtypes.bfloat16)


def pick_matrices():
    pick = np.zeros((2, 16, 64), np.float32)
    for which, width in ((0, 32), (1, 64)):
        for j in range(3):
            pick[which, j, j] = 1.0
        pick[which, 11, width - 2] = 1.0
        pick[which, 12, width - 1] = 1.0
    return pick.astype(ml_dtypes.bfloat16)


def place_matrix():
    place = np.zeros((8, 128), np.float32)
    for j in range(5):
        place[j, 64 + j] = 1.0
    return place


def face(mean, jump, k):
    q, u, t = mean[0], mean[1:4], mean[4]
    rho = jnp.exp(0.5 * q)
    speed = u[k]
    half_square = 0.5 * (u[0] * u[0] + u[1] * u[1] + u[2] * u[2])
    enthalpy = (1.0 / heat_ratio_less_one + 1.0) * t + half_square
    inner = jump[0] + jump[1] * u[0] + jump[2] * u[1] + jump[3] * u[2] + jump[4] * enthalpy
    flow = rho * speed
    grads = [flow * (jump[1 + j] + jump[4] * u[j]) for j in range(3)]
    grads[k] = grads[k] + rho * inner
    dq = 0.5 * (flow * inner + rho * t * jump[1 + k])
    dt = rho * jump[1 + k] + (1.0 / heat_ratio_less_one + 1.0) * flow * jump[4]
    return [dq] + grads + [dt]


def kernel(
    c_ref, x1_ref, y1_ref, x2_ref, y2_ref, sig_ref, adj_ref, ay_ref, ax_ref, pick_ref, place_ref,
    out_ref,
    tiles, mask_x, mask_y, ext, send_first, send_last, recv_first, recv_last,
    rows_low, rows_high, recv_low, recv_high,
    mapped, mapped_y2, state, edge, state_z,
    adj_ext, adj_edge, mid_ext, mid_edge,
    ax_send, ax_recv, ay_send, ay_recv, az_send, az_recv, gx_terms, gz_terms,
    send_sem, recv_sem,
):
    gx, gy, gz = lax.axis_index("gx"), lax.axis_index("gy"), lax.axis_index("gz")
    nx, ny = lax.axis_size("gx"), lax.axis_size("gy")
    x_up, x_down = {"gx": lax.rem(gx + 1, nx)}, {"gx": lax.rem(gx + nx - 1, nx)}
    y_up, y_down = {"gy": lax.rem(gy + 1, ny)}, {"gy": lax.rem(gy + ny - 1, ny)}
    z_other = {"gz": 1 - gz}
    barrier = pltpu.get_barrier_semaphore()
    for peer in (x_up, x_down, y_up, y_down, z_other):
        pl.semaphore_signal(barrier, inc=1, device_id=peer, device_id_type=MESH)

    def remote(index, source, target, peer):
        return pltpu.make_async_remote_copy(
            src_ref=source,
            dst_ref=target,
            send_sem=send_sem.at[index],
            recv_sem=recv_sem.at[index],
            device_id=peer,
            device_id_type=MESH,
        )

    lane = lax.broadcasted_iota(jnp.int32, (8, 128), 1)
    lane_wide = lax.broadcasted_iota(jnp.int32, (32, 128), 1)

    lane_tile = lax.broadcasted_iota(jnp.int32, (4, 64), 1) // 16
    row_half = lax.broadcasted_iota(jnp.int32, (8, 64), 0) < 4
    for c in range(2):
        for z in range(4):
            flags = sig_ref[c, z].astype(f32)
            wide = jnp.zeros((4, 64), f32)
            for t in range(4):
                wide = jnp.where(lane_tile == t, flags[:, t : t + 1], wide)
            tiles[c, z, 0:4] = wide
            each = [jnp.broadcast_to(tiles[c, z, t : t + 1], (8, 64)) for t in range(4)]
            for t in range(4):
                mask_y[c, z, 8 * t : 8 * t + 8] = each[t]
            for t in range(2):
                mask_x[c, z, 8 * t : 8 * t + 8] = jnp.where(row_half, each[2 * t], each[2 * t + 1])

    kept_x2 = x2_ref[...].astype(f32).reshape(2, 5, 4, 16, 64) * mask_x[...][:, None]
    kept_y2 = y2_ref[...].astype(f32).reshape(2, 5, 4, 32, 64) * mask_y[...][:, None]
    values = (
        c_ref[...],
        x1_ref[...],
        y1_ref[...],
        kept_x2.reshape(640, 64).astype(bf16),
        kept_y2.reshape(1280, 64).astype(bf16),
    )
    for (begin, end, width), value in zip(segments, values):
        pick = pick_ref[0 if width == 32 else 1][:, 0:width]
        ends = lax.dot_general(pick, value, (((1,), (1,)), ((), ())), preferred_element_type=f32)
        send_first[:, begin:end] = ends[0:8].astype(bf16)
        send_last[:, begin:end] = ends[8:16].astype(bf16)

    def pack_rims(source, which):
        for i in range(20):
            v, z = i // 4, i % 4
            ax_send[which, 0, i : i + 1] = source[v, z + 1, 8:9]
            ax_send[which, 1, i : i + 1] = source[v, z + 1, 39:40]
        first = jnp.zeros((32, 128), f32)
        last = jnp.zeros((32, 128), f32)
        for i in range(20):
            plane = source[i // 4, i % 4 + 1, 8:40]
            first = jnp.where(lane_wide == i, plane[:, 0:1], first)
            last = jnp.where(lane_wide == i, plane[:, 127:128], last)
        ay_send[which, 0] = first
        ay_send[which, 1] = last

    def rim_copies(source, which):
        base = 5 + 5 * which
        return [
            remote(base, ax_send.at[which, 0], ax_recv.at[which, 1], x_down),
            remote(base + 1, ax_send.at[which, 1], ax_recv.at[which, 0], x_up),
            remote(base + 2, ay_send.at[which, 0], ay_recv.at[which, 1], y_down),
            remote(base + 3, ay_send.at[which, 1], ay_recv.at[which, 0], y_up),
            remote(base + 4, source, az_recv.at[which], z_other),
        ]

    z_side = 3 - 3 * gz
    pl.semaphore_wait(barrier, 5)
    y_copies = [
        remote(0, send_first, recv_first, y_down),
        remote(1, send_last, recv_last, y_up),
    ]
    for copy in y_copies:
        copy.start()

    adj_ext[...] = jnp.zeros_like(adj_ext)
    for i in range(20):
        adj_ext[i // 4, i % 4 + 1, 8:40] = adj_ref[i // 4, i % 4]
    pack_rims(adj_ext, 0)
    adj_copies = rim_copies(adj_ref.at[:, z_side], 0)
    for copy in adj_copies:
        copy.start()

    ext[...] = jnp.zeros_like(ext)
    for (begin, end, width), value in zip(segments, values):
        ext[begin:end, 0:width] = value.astype(f32)
    mid_ext[...] = jnp.zeros_like(mid_ext)

    def fill_rims(target, target_edge, which):
        for i in range(20):
            v, z = i // 4, i % 4
            target[v, z + 1, 7:8] = ax_recv[which, 0, i : i + 1]
            target[v, z + 1, 40:41] = ax_recv[which, 1, i : i + 1]
            target_edge[v, z] = jnp.where(
                lane_wide == 0, ay_recv[which, 1, :, i : i + 1], ay_recv[which, 0, :, i : i + 1]
            )
        for v in range(5):
            plane = az_recv[which, v]
            target[v, 0, 8:40] = jnp.where(gz > 0, plane, 0.0)
            target[v, 5, 8:40] = jnp.where(gz > 0, 0.0, plane)

    for copy in y_copies:
        copy.wait()
    joined = recv_first[...].astype(f32) + recv_last[...].astype(f32)
    ext[...] += jnp.dot(joined.T, place_ref[...], preferred_element_type=f32)

    coarse_e = ext[0:320].reshape(40, 8, 128)
    x1_e = ext[320:640].reshape(40, 8, 128)
    y1_e = ext[640:1280].reshape(40, 16, 128)
    x2_e = ext[1280:1920].reshape(40, 16, 128)
    y2_e = ext[1920:3200].reshape(40, 32, 128)
    blank = jnp.zeros((40, 1, 128), f32)
    low = jnp.concatenate(
        [coarse_e[:, 6:8], x1_e[:, 7:8], y1_e[:, 14:16], x2_e[:, 15:16], y2_e[:, 31:32], blank], 1
    )
    high = jnp.concatenate(
        [coarse_e[:, 0:3], x1_e[:, 0:1], y1_e[:, 0:2], y2_e[:, 0:1], blank], 1
    )
    rows_low[...] = low.reshape(320, 128).astype(bf16)
    rows_high[...] = high.reshape(320, 128).astype(bf16)
    x_copies = [
        remote(2, rows_low, recv_low, x_up),
        remote(3, rows_high, recv_high, x_down),
    ]
    for copy in x_copies:
        copy.start()

    for (begin, end, width), which, at in zip(segments, (0, 0, 1, 2, 3), (0, 8, 16, 32, None)):
        product = jnp.dot(
            ext[begin:end].astype(bf16), ay_ref[which], preferred_element_type=f32
        ).reshape(40, (end - begin) // 40, 256)
        if at is None:
            mapped_y2[...] = product
        else:
            mapped[:, at : at + (end - begin) // 40] = product

    for copy in adj_copies:
        copy.wait()
    fill_rims(adj_ext, adj_edge, 0)

    row_kind = lax.broadcasted_iota(jnp.int32, (320, 128), 0) % 8
    for copy in x_copies:
        copy.wait()
    for buffer, at, bounds in (
        (recv_low, 48, ((0, 3), (3, 5), (5, 6), (6, 8))),
        (recv_high, 56, ((0, 4), (4, 6), (6, 6), (6, 8))),
    ):
        received = buffer[...].astype(f32)
        total = jnp.zeros((320, 256), f32)
        for which, (begin, end) in enumerate(bounds):
            if begin < end:
                part = jnp.where((row_kind >= begin) & (row_kind < end), received, 0.0)
                total = total + jnp.dot(
                    part.astype(bf16), ay_ref[which], preferred_element_type=f32
                )
        mapped[:, at : at + 8] = total.reshape(40, 8, 256)

    def synthesize(cv, carry):
        for z in range(4):
            p = cv * 4 + z
            exact = mapped[p]
            coarse_bits = exact.astype(bf16)
            rest = (exact - coarse_bits.astype(f32)).astype(bf16)
            whole = jnp.dot(
                ax_ref[...],
                jnp.concatenate([coarse_bits, rest], axis=0),
                preferred_element_type=f32,
            )
            extra = mapped_y2[p]
            state[cv, z + 1, 0:8] = whole[0:8, 0:128]
            state[cv, z + 1, 8:40] = whole[8:40, 0:128] + extra[:, 0:128]
            state[cv, z + 1, 40:48] = whole[40:48, 0:128]
            edge[cv, z] = whole[8:40, 128:256] + extra[:, 128:256]
        return carry

    lax.fori_loop(0, 10, synthesize, 0)
    state_copy = remote(4, state.at[:, z_side + 1, 8:40], state_z, z_other)
    state_copy.start()
    state_copy.wait()
    for cv in range(10):
        plane = state_z[cv]
        state[cv, 0, 8:40] = jnp.where(gz > 0, plane, 0.0)
        state[cv, 5, 8:40] = jnp.where(gz > 0, 0.0, plane)

    keep_bottom = jnp.where(gz > 0, 1.0, 0.0).astype(f32)

    def rate(base, source, source_edge, finish):
        def z_faces(k, carry):
            for r in range(4):
                at = slice(8 + 8 * r, 16 + 8 * r)
                mean = [0.5 * (state[base + v, k, at] + state[base + v, k + 1, at]) for v in range(5)]
                jump = [source[v, k + 1, at] - source[v, k, at] for v in range(5)]
                terms = face(mean, jump, 2)
                factor = jnp.where(k == 0, keep_bottom, 1.0)
                for v in range(5):
                    gz_terms[v, k, 8 * r : 8 * r + 8] = terms[v] * factor
            return carry

        lax.fori_loop(0, 5, z_faces, 0)

        def plane(z, carry):
            for r in range(5):
                low_at, high_at = slice(7 + 8 * r, 15 + 8 * r), slice(8 + 8 * r, 16 + 8 * r)
                mean = [
                    0.5 * (state[base + v, z + 1, low_at] + state[base + v, z + 1, high_at])
                    for v in range(5)
                ]
                jump = [source[v, z + 1, high_at] - source[v, z + 1, low_at] for v in range(5)]
                terms = face(mean, jump, 0)
                for v in range(5):
                    gx_terms[v, 8 * r : 8 * r + 8] = terms[v]
            for r in range(4):
                at, rows = slice(8 + 8 * r, 16 + 8 * r), slice(8 * r, 8 * r + 8)
                here = [state[base + v, z + 1, at] for v in range(5)]
                rim = [edge[base + v, z, rows] for v in range(5)]
                adj = [source[v, z + 1, at] for v in range(5)]
                adj_rim = [source_edge[v, z, rows] for v in range(5)]

                def ahead(a, b):
                    return pltpu.roll(jnp.where(lane == 0, b, a), 127, 1)

                def behind(a, b):
                    return pltpu.roll(jnp.where(lane == 127, b, a), 1, 1)

                adj_up = [ahead(adj[v], adj_rim[v]) for v in range(5)]
                adj_down = [behind(adj[v], adj_rim[v]) for v in range(5)]
                up = face(
                    [0.5 * (here[v] + ahead(here[v], rim[v])) for v in range(5)],
                    [adj_up[v] - adj[v] for v in range(5)],
                    1,
                )
                down = face(
                    [0.5 * (here[v] + behind(here[v], rim[v])) for v in range(5)],
                    [adj[v] - adj_down[v] for v in range(5)],
                    1,
                )
                for v in range(5):
                    halves = (
                        up[v]
                        + down[v]
                        + gx_terms[v, rows]
                        + gx_terms[v, 8 * r + 1 : 8 * r + 9]
                        + gz_terms[v, z, rows]
                        + gz_terms[v, z + 1, rows]
                    )
                    around = (
                        adj_up[v]
                        + adj_down[v]
                        + source[v, z + 1, 7 + 8 * r : 15 + 8 * r]
                        + source[v, z + 1, 9 + 8 * r : 17 + 8 * r]
                        + source[v, z, at]
                        + source[v, z + 2, at]
                    )
                    finish(v, z, rows, at, 0.5 * halves + viscosity * (around - 6.0 * adj[v]))
            return carry

        lax.fori_loop(0, 4, plane, 0)

    def finish_first(v, z, rows, at, value):
        held = adj_ext[v, z + 1, at]
        mid_ext[v, z + 1, at] = held + time_step * value
        out_ref[v, z, rows] = held + 0.5 * time_step * value

    def finish_second(v, z, rows, at, value):
        out_ref[v, z, rows] += 0.5 * time_step * value

    rate(0, adj_ext, adj_edge, finish_first)
    pack_rims(mid_ext, 1)
    mid_copies = rim_copies(mid_ext.at[:, z_side + 1, 8:40], 1)
    for copy in mid_copies:
        copy.start()
    for copy in mid_copies:
        copy.wait()
    fill_rims(mid_ext, mid_edge, 1)
    rate(5, mid_ext, mid_edge, finish_second)


def shards(coarse, detail_x1, detail_y1, detail_x2, detail_y2, significance, adjoint):
    vmem = pl.BlockSpec(memory_space=pltpu.VMEM)
    return pl.pallas_call(
        kernel,
        out_shape=jax.ShapeDtypeStruct(adjoint.shape, f32),
        in_specs=[vmem] * 11,
        out_specs=vmem,
        scratch_shapes=[
            pltpu.VMEM((2, 4, 8, 64), f32),
            pltpu.VMEM((2, 4, 16, 64), f32),
            pltpu.VMEM((2, 4, 32, 64), f32),
            pltpu.VMEM((3200, 128), f32),
            pltpu.VMEM((8, 3200), bf16),
            pltpu.VMEM((8, 3200), bf16),
            pltpu.VMEM((8, 3200), bf16),
            pltpu.VMEM((8, 3200), bf16),
            pltpu.VMEM((320, 128), bf16),
            pltpu.VMEM((320, 128), bf16),
            pltpu.VMEM((320, 128), bf16),
            pltpu.VMEM((320, 128), bf16),
            pltpu.VMEM((40, 64, 256), f32),
            pltpu.VMEM((40, 32, 256), f32),
            pltpu.VMEM((10, 6, 48, 128), f32),
            pltpu.VMEM((10, 4, 32, 128), f32),
            pltpu.VMEM((10, 32, 128), f32),
            pltpu.VMEM((5, 6, 48, 128), f32),
            pltpu.VMEM((5, 4, 32, 128), f32),
            pltpu.VMEM((5, 6, 48, 128), f32),
            pltpu.VMEM((5, 4, 32, 128), f32),
            pltpu.VMEM((2, 2, 24, 128), f32),
            pltpu.VMEM((2, 2, 24, 128), f32),
            pltpu.VMEM((2, 2, 32, 128), f32),
            pltpu.VMEM((2, 2, 32, 128), f32),
            pltpu.VMEM((8, 128), f32),
            pltpu.VMEM((2, 5, 32, 128), f32),
            pltpu.VMEM((5, 40, 128), f32),
            pltpu.VMEM((5, 5, 32, 128), f32),
            pltpu.SemaphoreType.DMA((15,)),
            pltpu.SemaphoreType.DMA((15,)),
        ],
        compiler_params=pltpu.CompilerParams(collective_id=0, has_side_effects=True),
    )(
        coarse.reshape(320, 32),
        detail_x1.reshape(320, 32),
        detail_y1.reshape(640, 32),
        detail_x2.reshape(640, 64),
        detail_y2.reshape(1280, 64),
        significance,
        adjoint,
        jnp.asarray(y_matrices()),
        jnp.asarray(x_matrix()),
        jnp.asarray(pick_matrices()),
        jnp.asarray(place_matrix()),
    )


def solution(mesh):
    return jax.shard_map(
        shards,
        mesh=mesh,
        in_specs=(
            P(None, None, "gz", "gx", "gy"),
            P(None, None, "gz", "gx", "gy"),
            P(None, None, "gz", "gx", "gy"),
            P(None, None, "gz", "gx", "gy"),
            P(None, None, "gz", "gx", "gy"),
            P(None, "gz", "gx", "gy"),
            P(None, "gz", "gx", "gy"),
        ),
        out_specs=P(None, "gz", "gx", "gy"),
        check_vma=False,
    )
```

```python
import functools

import jax
import jax.numpy as jnp
import ml_dtypes
import numpy as np
from jax import lax
from jax.experimental import pallas as pl
from jax.experimental.pallas import tpu as pltpu
from jax.sharding import PartitionSpec as P

time_step = 0.1
viscosity = 0.2
heat_ratio_less_one = 0.4
f32 = jnp.float32
bf16 = jnp.bfloat16
MESH = pl.DeviceIdType.MESH
segments = ((0, 320, 32), (320, 640, 32), (640, 1280, 32), (1280, 1920, 64), (1920, 3200, 64))


def predict(index):
    k = index // 2
    if index % 2 == 0:
        return {("c", k): 1.0}
    return {
        ("d", k): 1.0,
        ("c", k): 9 / 16,
        ("c", k + 1): 9 / 16,
        ("c", k - 1): -1 / 16,
        ("c", k + 2): -1 / 16,
    }


def predict_twice(index):
    whole = {}
    for (kind, k), weight in predict(index).items():
        if kind == "d":
            whole[("e", k)] = weight
            continue
        whole[("m", k)] = weight
        for key, inner in predict(k).items():
            whole[key] = whole.get(key, 0.0) + weight * inner
    return whole


def lane_of(k, length):
    if k < 0:
        return 69 + k
    return k if k < length else 64 + k - length


def y_matrices():
    mats = np.zeros((4, 128, 256), np.float32)
    columns = [(y, y) for y in range(128)] + [(128, 128), (-1, 255)]
    for y, column in columns:
        for (kind, k), weight in predict_twice(y).items():
            which = "cdme".index(kind)
            mats[which, lane_of(k, 32 if which < 2 else 64), column] += weight
    return mats.astype(ml_dtypes.bfloat16)


def x_matrix():
    mat = np.zeros((48, 64), np.float32)
    for x in range(-1, 33):
        row = x + 8
        for (kind, k), weight in predict_twice(x).items():
            if kind == "c":
                at = 50 + k if k < 0 else (k if k < 8 else 56 + k - 8)
            elif kind == "d":
                at = 50 if k < 0 else (8 + k if k < 8 else 59)
            elif kind == "m":
                at = 53 + k if k < 0 else (16 + k if k < 16 else 60 + k - 16)
            else:
                at = 53 if k < 0 else 32 + k
            mat[row, at] += weight
    mat[7, 54] = 1.0
    mat[40, 62] = 1.0
    return np.concatenate([mat, mat], axis=1).astype(ml_dtypes.bfloat16)


def pick_matrices():
    pick = np.zeros((2, 16, 64), np.float32)
    for which, width in ((0, 32), (1, 64)):
        for j in range(3):
            pick[which, j, j] = 1.0
        pick[which, 11, width - 2] = 1.0
        pick[which, 12, width - 1] = 1.0
    return pick.astype(ml_dtypes.bfloat16)


def place_matrix():
    place = np.zeros((8, 128), np.float32)
    for j in range(5):
        place[j, 64 + j] = 1.0
    return place


def face(mean, jump, k):
    q, u, t = mean[0], mean[1:4], mean[4]
    rho = jnp.exp(0.5 * q)
    speed = u[k]
    half_square = 0.5 * (u[0] * u[0] + u[1] * u[1] + u[2] * u[2])
    enthalpy = (1.0 / heat_ratio_less_one + 1.0) * t + half_square
    inner = jump[0] + jump[1] * u[0] + jump[2] * u[1] + jump[3] * u[2] + jump[4] * enthalpy
    flow = rho * speed
    grads = [flow * (jump[1 + j] + jump[4] * u[j]) for j in range(3)]
    grads[k] = grads[k] + rho * inner
    dq = 0.5 * (flow * inner + rho * t * jump[1 + k])
    dt = rho * jump[1 + k] + (1.0 / heat_ratio_less_one + 1.0) * flow * jump[4]
    return [dq] + grads + [dt]


def kernel(
    c_in, x1_in, y1_in, x2_in, y2_in, sig_in, adj_in, ay_in, ax_in, pick_in, place_in,
    out_any,
    c_ref, x1_ref, y1_ref, x2_ref, y2_ref, sig_ref, adj_ref, ay_ref, ax_ref, pick_ref, place_ref,
    out_ref, load_sem,
    tiles, mask_x, mask_y, ext, send_first, send_last, recv_first, recv_last,
    rows_low, rows_high, recv_low, recv_high,
    mapped, mapped_y2, state, edge, state_z,
    adj_ext, adj_edge, mid_ext, mid_edge,
    ax_send, ax_recv, ay_send, ay_recv, az_send, az_recv, gx_terms, gz_terms,
    send_sem, recv_sem,
):
    gx, gy, gz = lax.axis_index("gx"), lax.axis_index("gy"), lax.axis_index("gz")
    nx, ny = lax.axis_size("gx"), lax.axis_size("gy")
    x_up, x_down = {"gx": lax.rem(gx + 1, nx)}, {"gx": lax.rem(gx + nx - 1, nx)}
    y_up, y_down = {"gy": lax.rem(gy + 1, ny)}, {"gy": lax.rem(gy + ny - 1, ny)}
    z_other = {"gz": 1 - gz}
    barrier = pltpu.get_barrier_semaphore()
    for peer in (x_up, x_down, y_up, y_down, z_other):
        pl.semaphore_signal(barrier, inc=1, device_id=peer, device_id_type=MESH)

    pairs = (
        (sig_in, sig_ref), (x2_in, x2_ref), (y2_in, y2_ref), (c_in, c_ref), (x1_in, x1_ref),
        (y1_in, y1_ref), (pick_in, pick_ref), (adj_in, adj_ref), (place_in, place_ref),
        (ay_in, ay_ref), (ax_in, ax_ref),
    )
    loads = [
        pltpu.make_async_copy(source, target, load_sem.at[i])
        for i, (source, target) in enumerate(pairs)
    ]
    for load in loads:
        load.start()

    def remote(index, source, target, peer):
        return pltpu.make_async_remote_copy(
            src_ref=source,
            dst_ref=target,
            send_sem=send_sem.at[index],
            recv_sem=recv_sem.at[index],
            device_id=peer,
            device_id_type=MESH,
        )

    lane = lax.broadcasted_iota(jnp.int32, (8, 128), 1)
    lane_wide = lax.broadcasted_iota(jnp.int32, (32, 128), 1)

    for load in loads[:7]:
        load.wait()
    lane_tile = lax.broadcasted_iota(jnp.int32, (4, 64), 1) // 16
    row_half = lax.broadcasted_iota(jnp.int32, (8, 64), 0) < 4
    for c in range(2):
        for z in range(4):
            flags = sig_ref[c, z].astype(f32)
            wide = jnp.zeros((4, 64), f32)
            for t in range(4):
                wide = jnp.where(lane_tile == t, flags[:, t : t + 1], wide)
            tiles[c, z, 0:4] = wide
            each = [jnp.broadcast_to(tiles[c, z, t : t + 1], (8, 64)) for t in range(4)]
            for t in range(4):
                mask_y[c, z, 8 * t : 8 * t + 8] = each[t]
            for t in range(2):
                mask_x[c, z, 8 * t : 8 * t + 8] = jnp.where(row_half, each[2 * t], each[2 * t + 1])

    kept_x2 = x2_ref[...].astype(f32).reshape(2, 5, 4, 16, 64) * mask_x[...][:, None]
    kept_y2 = y2_ref[...].astype(f32).reshape(2, 5, 4, 32, 64) * mask_y[...][:, None]
    values = (
        c_ref[...],
        x1_ref[...],
        y1_ref[...],
        kept_x2.reshape(640, 64).astype(bf16),
        kept_y2.reshape(1280, 64).astype(bf16),
    )
    for (begin, end, width), value in zip(segments, values):
        pick = pick_ref[0 if width == 32 else 1][:, 0:width]
        ends = lax.dot_general(pick, value, (((1,), (1,)), ((), ())), preferred_element_type=f32)
        send_first[:, begin:end] = ends[0:8].astype(bf16)
        send_last[:, begin:end] = ends[8:16].astype(bf16)

    def pack_rims(source, which):
        for i in range(20):
            v, z = i // 4, i % 4
            ax_send[which, 0, i : i + 1] = source[v, z + 1, 8:9]
            ax_send[which, 1, i : i + 1] = source[v, z + 1, 39:40]
        first = jnp.zeros((32, 128), f32)
        last = jnp.zeros((32, 128), f32)
        for i in range(20):
            plane = source[i // 4, i % 4 + 1, 8:40]
            first = jnp.where(lane_wide == i, plane[:, 0:1], first)
            last = jnp.where(lane_wide == i, plane[:, 127:128], last)
        ay_send[which, 0] = first
        ay_send[which, 1] = last

    def rim_copies(source, which):
        base = 5 + 5 * which
        return [
            remote(base, ax_send.at[which, 0], ax_recv.at[which, 1], x_down),
            remote(base + 1, ax_send.at[which, 1], ax_recv.at[which, 0], x_up),
            remote(base + 2, ay_send.at[which, 0], ay_recv.at[which, 1], y_down),
            remote(base + 3, ay_send.at[which, 1], ay_recv.at[which, 0], y_up),
            remote(base + 4, source, az_recv.at[which], z_other),
        ]

    z_side = 3 - 3 * gz
    pl.semaphore_wait(barrier, 5)
    y_copies = [
        remote(0, send_first, recv_first, y_down),
        remote(1, send_last, recv_last, y_up),
    ]
    for copy in y_copies:
        copy.start()

    loads[7].wait()
    adj_ext[...] = jnp.zeros_like(adj_ext)
    for i in range(20):
        adj_ext[i // 4, i % 4 + 1, 8:40] = adj_ref[i // 4, i % 4]
    pack_rims(adj_ext, 0)
    adj_copies = rim_copies(adj_ref.at[:, z_side], 0)
    for copy in adj_copies:
        copy.start()

    ext[...] = jnp.zeros_like(ext)
    for (begin, end, width), value in zip(segments, values):
        ext[begin:end, 0:width] = value.astype(f32)
    mid_ext[...] = jnp.zeros_like(mid_ext)

    def fill_rims(target, target_edge, which):
        for i in range(20):
            v, z = i // 4, i % 4
            target[v, z + 1, 7:8] = ax_recv[which, 0, i : i + 1]
            target[v, z + 1, 40:41] = ax_recv[which, 1, i : i + 1]
            target_edge[v, z] = jnp.where(
                lane_wide == 0, ay_recv[which, 1, :, i : i + 1], ay_recv[which, 0, :, i : i + 1]
            )
        for v in range(5):
            plane = az_recv[which, v]
            target[v, 0, 8:40] = jnp.where(gz > 0, plane, 0.0)
            target[v, 5, 8:40] = jnp.where(gz > 0, 0.0, plane)

    for load in loads[8:]:
        load.wait()
    for copy in y_copies:
        copy.wait()
    joined = recv_first[...].astype(f32) + recv_last[...].astype(f32)
    ext[...] += jnp.dot(joined.T, place_ref[...], preferred_element_type=f32)

    coarse_e = ext[0:320].reshape(40, 8, 128)
    x1_e = ext[320:640].reshape(40, 8, 128)
    y1_e = ext[640:1280].reshape(40, 16, 128)
    x2_e = ext[1280:1920].reshape(40, 16, 128)
    y2_e = ext[1920:3200].reshape(40, 32, 128)
    blank = jnp.zeros((40, 1, 128), f32)
    low = jnp.concatenate(
        [coarse_e[:, 6:8], x1_e[:, 7:8], y1_e[:, 14:16], x2_e[:, 15:16], y2_e[:, 31:32], blank], 1
    )
    high = jnp.concatenate(
        [coarse_e[:, 0:3], x1_e[:, 0:1], y1_e[:, 0:2], y2_e[:, 0:1], blank], 1
    )
    rows_low[...] = low.reshape(320, 128).astype(bf16)
    rows_high[...] = high.reshape(320, 128).astype(bf16)
    x_copies = [
        remote(2, rows_low, recv_low, x_up),
        remote(3, rows_high, recv_high, x_down),
    ]
    for copy in x_copies:
        copy.start()

    for (begin, end, width), which, at in zip(segments, (0, 0, 1, 2, 3), (0, 8, 16, 32, None)):
        product = jnp.dot(
            ext[begin:end].astype(bf16), ay_ref[which], preferred_element_type=f32
        ).reshape(40, (end - begin) // 40, 256)
        if at is None:
            mapped_y2[...] = product
        else:
            mapped[:, at : at + (end - begin) // 40] = product

    for copy in adj_copies:
        copy.wait()
    fill_rims(adj_ext, adj_edge, 0)

    row_kind = lax.broadcasted_iota(jnp.int32, (320, 128), 0) % 8
    for copy in x_copies:
        copy.wait()
    for buffer, at, bounds in (
        (recv_low, 48, ((0, 3), (3, 5), (5, 6), (6, 8))),
        (recv_high, 56, ((0, 4), (4, 6), (6, 6), (6, 8))),
    ):
        received = buffer[...].astype(f32)
        total = jnp.zeros((320, 256), f32)
        for which, (begin, end) in enumerate(bounds):
            if begin < end:
                part = jnp.where((row_kind >= begin) & (row_kind < end), received, 0.0)
                total = total + jnp.dot(
                    part.astype(bf16), ay_ref[which], preferred_element_type=f32
                )
        mapped[:, at : at + 8] = total.reshape(40, 8, 256)

    def synthesize(order, cv, carry):
        for z in order:
            p = cv * 4 + z
            exact = mapped[p]
            coarse_bits = exact.astype(bf16)
            rest = (exact - coarse_bits.astype(f32)).astype(bf16)
            whole = jnp.dot(
                ax_ref[...],
                jnp.concatenate([coarse_bits, rest], axis=0),
                preferred_element_type=f32,
            )
            extra = mapped_y2[p]
            state[cv, z + 1, 0:8] = whole[0:8, 0:128]
            state[cv, z + 1, 8:40] = whole[8:40, 0:128] + extra[:, 0:128]
            state[cv, z + 1, 40:48] = whole[40:48, 0:128]
            edge[cv, z] = whole[8:40, 128:256] + extra[:, 128:256]
        return carry

    def synthesize_sides(pair, carry):
        for j in range(5):
            synthesize((z_side,), 5 * pair + j, carry)
        return carry

    lax.fori_loop(0, 2, synthesize_sides, 0)
    state_copy = remote(4, state.at[:, z_side + 1, 8:40], state_z, z_other)
    state_copy.start()
    lax.fori_loop(0, 10, functools.partial(synthesize, (gz, gz + 1, gz + 2)), 0)
    state_copy.wait()
    for cv in range(10):
        plane = state_z[cv]
        state[cv, 0, 8:40] = jnp.where(gz > 0, plane, 0.0)
        state[cv, 5, 8:40] = jnp.where(gz > 0, 0.0, plane)

    keep_bottom = jnp.where(gz > 0, 1.0, 0.0).astype(f32)

    def rate(base, source, source_edge, finish):
        def z_faces(k, carry):
            for r in range(4):
                at = slice(8 + 8 * r, 16 + 8 * r)
                mean = [0.5 * (state[base + v, k, at] + state[base + v, k + 1, at]) for v in range(5)]
                jump = [source[v, k + 1, at] - source[v, k, at] for v in range(5)]
                terms = face(mean, jump, 2)
                factor = jnp.where(k == 0, keep_bottom, 1.0)
                for v in range(5):
                    gz_terms[v, k, 8 * r : 8 * r + 8] = terms[v] * factor
            return carry

        lax.fori_loop(0, 5, z_faces, 0)

        def plane(z, carry):
            for r in range(5):
                low_at, high_at = slice(7 + 8 * r, 15 + 8 * r), slice(8 + 8 * r, 16 + 8 * r)
                mean = [
                    0.5 * (state[base + v, z + 1, low_at] + state[base + v, z + 1, high_at])
                    for v in range(5)
                ]
                jump = [source[v, z + 1, high_at] - source[v, z + 1, low_at] for v in range(5)]
                terms = face(mean, jump, 0)
                for v in range(5):
                    gx_terms[v, 8 * r : 8 * r + 8] = terms[v]
            for r in range(4):
                at, rows = slice(8 + 8 * r, 16 + 8 * r), slice(8 * r, 8 * r + 8)
                here = [state[base + v, z + 1, at] for v in range(5)]
                rim = [edge[base + v, z, rows] for v in range(5)]
                adj = [source[v, z + 1, at] for v in range(5)]
                adj_rim = [source_edge[v, z, rows] for v in range(5)]

                def ahead(a, b):
                    return pltpu.roll(jnp.where(lane == 0, b, a), 127, 1)

                def behind(a, b):
                    return pltpu.roll(jnp.where(lane == 127, b, a), 1, 1)

                adj_up = [ahead(adj[v], adj_rim[v]) for v in range(5)]
                adj_down = [behind(adj[v], adj_rim[v]) for v in range(5)]
                up = face(
                    [0.5 * (here[v] + ahead(here[v], rim[v])) for v in range(5)],
                    [adj_up[v] - adj[v] for v in range(5)],
                    1,
                )
                down = face(
                    [0.5 * (here[v] + behind(here[v], rim[v])) for v in range(5)],
                    [adj[v] - adj_down[v] for v in range(5)],
                    1,
                )
                for v in range(5):
                    halves = (
                        up[v]
                        + down[v]
                        + gx_terms[v, rows]
                        + gx_terms[v, 8 * r + 1 : 8 * r + 9]
                        + gz_terms[v, z, rows]
                        + gz_terms[v, z + 1, rows]
                    )
                    around = (
                        adj_up[v]
                        + adj_down[v]
                        + source[v, z + 1, 7 + 8 * r : 15 + 8 * r]
                        + source[v, z + 1, 9 + 8 * r : 17 + 8 * r]
                        + source[v, z, at]
                        + source[v, z + 2, at]
                    )
                    finish(v, z, rows, at, 0.5 * halves + viscosity * (around - 6.0 * adj[v]))
            return carry

        lax.fori_loop(0, 4, plane, 0)

    def finish_first(v, z, rows, at, value):
        held = adj_ext[v, z + 1, at]
        mid_ext[v, z + 1, at] = held + time_step * value
        out_ref[v, z, rows] = held + 0.5 * time_step * value

    def finish_second(v, z, rows, at, value):
        out_ref[v, z, rows] += 0.5 * time_step * value

    rate(0, adj_ext, adj_edge, finish_first)
    pack_rims(mid_ext, 1)
    mid_copies = rim_copies(mid_ext.at[:, z_side + 1, 8:40], 1)
    for copy in mid_copies:
        copy.start()
    for copy in mid_copies:
        copy.wait()
    fill_rims(mid_ext, mid_edge, 1)
    rate(5, mid_ext, mid_edge, finish_second)
    store = pltpu.make_async_copy(out_ref, out_any, load_sem.at[11])
    store.start()
    store.wait()


def shards(coarse, detail_x1, detail_y1, detail_x2, detail_y2, significance, adjoint):
    anywhere = pl.BlockSpec(memory_space=pl.ANY)
    return pl.pallas_call(
        kernel,
        out_shape=jax.ShapeDtypeStruct(adjoint.shape, f32),
        in_specs=[pl.BlockSpec(memory_space=pltpu.HBM)] * 11,
        out_specs=anywhere,
        scratch_shapes=[
            pltpu.VMEM((320, 32), bf16),
            pltpu.VMEM((320, 32), bf16),
            pltpu.VMEM((640, 32), bf16),
            pltpu.VMEM((640, 64), bf16),
            pltpu.VMEM((1280, 64), bf16),
            pltpu.VMEM((2, 4, 4, 4), jnp.int32),
            pltpu.VMEM((5, 4, 32, 128), f32),
            pltpu.VMEM((4, 128, 256), bf16),
            pltpu.VMEM((48, 128), bf16),
            pltpu.VMEM((2, 16, 64), bf16),
            pltpu.VMEM((8, 128), f32),
            pltpu.VMEM((5, 4, 32, 128), f32),
            pltpu.SemaphoreType.DMA((12,)),
            pltpu.VMEM((2, 4, 8, 64), f32),
            pltpu.VMEM((2, 4, 16, 64), f32),
            pltpu.VMEM((2, 4, 32, 64), f32),
            pltpu.VMEM((3200, 128), f32),
            pltpu.VMEM((8, 3200), bf16),
            pltpu.VMEM((8, 3200), bf16),
            pltpu.VMEM((8, 3200), bf16),
            pltpu.VMEM((8, 3200), bf16),
            pltpu.VMEM((320, 128), bf16),
            pltpu.VMEM((320, 128), bf16),
            pltpu.VMEM((320, 128), bf16),
            pltpu.VMEM((320, 128), bf16),
            pltpu.VMEM((40, 64, 256), f32),
            pltpu.VMEM((40, 32, 256), f32),
            pltpu.VMEM((10, 6, 48, 128), f32),
            pltpu.VMEM((10, 4, 32, 128), f32),
            pltpu.VMEM((10, 32, 128), f32),
            pltpu.VMEM((5, 6, 48, 128), f32),
            pltpu.VMEM((5, 4, 32, 128), f32),
            pltpu.VMEM((5, 6, 48, 128), f32),
            pltpu.VMEM((5, 4, 32, 128), f32),
            pltpu.VMEM((2, 2, 24, 128), f32),
            pltpu.VMEM((2, 2, 24, 128), f32),
            pltpu.VMEM((2, 2, 32, 128), f32),
            pltpu.VMEM((2, 2, 32, 128), f32),
            pltpu.VMEM((8, 128), f32),
            pltpu.VMEM((2, 5, 32, 128), f32),
            pltpu.VMEM((5, 40, 128), f32),
            pltpu.VMEM((5, 5, 32, 128), f32),
            pltpu.SemaphoreType.DMA((15,)),
            pltpu.SemaphoreType.DMA((15,)),
        ],
        compiler_params=pltpu.CompilerParams(collective_id=0, has_side_effects=True, vmem_limit_bytes=24*1024*1024),
    )(
        coarse.reshape(320, 32),
        detail_x1.reshape(320, 32),
        detail_y1.reshape(640, 32),
        detail_x2.reshape(640, 64),
        detail_y2.reshape(1280, 64),
        significance,
        adjoint,
        jnp.asarray(y_matrices()),
        jnp.asarray(x_matrix()),
        jnp.asarray(pick_matrices()),
        jnp.asarray(place_matrix()),
    )


def solution(mesh):
    return jax.shard_map(
        shards,
        mesh=mesh,
        in_specs=(
            P(None, None, "gz", "gx", "gy"),
            P(None, None, "gz", "gx", "gy"),
            P(None, None, "gz", "gx", "gy"),
            P(None, None, "gz", "gx", "gy"),
            P(None, None, "gz", "gx", "gy"),
            P(None, "gz", "gx", "gy"),
            P(None, "gz", "gx", "gy"),
        ),
        out_specs=P(None, "gz", "gx", "gy"),
        check_vma=False,
    )
```

```python
import functools

import jax
import jax.numpy as jnp
import ml_dtypes
import numpy as np
from jax import lax
from jax.experimental import pallas as pl
from jax.experimental.pallas import tpu as pltpu
from jax.sharding import PartitionSpec as P

time_step = 0.1
viscosity = 0.2
heat_ratio_less_one = 0.4
f32 = jnp.float32
bf16 = jnp.bfloat16
MESH = pl.DeviceIdType.MESH
segments = ((0, 320, 32), (320, 640, 32), (640, 1280, 32), (1280, 1920, 64), (1920, 3200, 64))


def predict(index):
    k = index // 2
    if index % 2 == 0:
        return {("c", k): 1.0}
    return {
        ("d", k): 1.0,
        ("c", k): 9 / 16,
        ("c", k + 1): 9 / 16,
        ("c", k - 1): -1 / 16,
        ("c", k + 2): -1 / 16,
    }


def predict_twice(index):
    whole = {}
    for (kind, k), weight in predict(index).items():
        if kind == "d":
            whole[("e", k)] = weight
            continue
        whole[("m", k)] = weight
        for key, inner in predict(k).items():
            whole[key] = whole.get(key, 0.0) + weight * inner
    return whole


def lane_of(k, length):
    if k < 0:
        return 69 + k
    return k if k < length else 64 + k - length


def y_matrices():
    mats = np.zeros((4, 128, 256), np.float32)
    columns = [(y, y) for y in range(128)] + [(128, 128), (-1, 255)]
    for y, column in columns:
        for (kind, k), weight in predict_twice(y).items():
            which = "cdme".index(kind)
            mats[which, lane_of(k, 32 if which < 2 else 64), column] += weight
    return mats.astype(ml_dtypes.bfloat16)


def x_matrix():
    mat = np.zeros((48, 64), np.float32)
    for x in range(-1, 33):
        row = x + 8
        for (kind, k), weight in predict_twice(x).items():
            if kind == "c":
                at = 50 + k if k < 0 else (k if k < 8 else 56 + k - 8)
            elif kind == "d":
                at = 50 if k < 0 else (8 + k if k < 8 else 59)
            elif kind == "m":
                at = 53 + k if k < 0 else (16 + k if k < 16 else 60 + k - 16)
            else:
                at = 53 if k < 0 else 32 + k
            mat[row, at] += weight
    mat[7, 54] = 1.0
    mat[40, 62] = 1.0
    return np.concatenate([mat, mat], axis=1).astype(ml_dtypes.bfloat16)


def pick_matrices():
    pick = np.zeros((2, 16, 64), np.float32)
    for which, width in ((0, 32), (1, 64)):
        for j in range(3):
            pick[which, j, j] = 1.0
        pick[which, 11, width - 2] = 1.0
        pick[which, 12, width - 1] = 1.0
    return pick.astype(ml_dtypes.bfloat16)


def place_matrix():
    place = np.zeros((8, 128), np.float32)
    for j in range(5):
        place[j, 64 + j] = 1.0
    return place


def face(mean, jump, k):
    q, u, t = mean[0], mean[1:4], mean[4]
    rho = jnp.exp(0.5 * q)
    speed = u[k]
    half_square = 0.5 * (u[0] * u[0] + u[1] * u[1] + u[2] * u[2])
    enthalpy = (1.0 / heat_ratio_less_one + 1.0) * t + half_square
    inner = jump[0] + jump[1] * u[0] + jump[2] * u[1] + jump[3] * u[2] + jump[4] * enthalpy
    flow = rho * speed
    grads = [flow * (jump[1 + j] + jump[4] * u[j]) for j in range(3)]
    grads[k] = grads[k] + rho * inner
    dq = 0.5 * (flow * inner + rho * t * jump[1 + k])
    dt = rho * jump[1 + k] + (1.0 / heat_ratio_less_one + 1.0) * flow * jump[4]
    return [dq] + grads + [dt]


def kernel(
    c_in, x1_in, y1_in, x2_in, y2_in, sig_in, adj_in, ay_in, ax_in, pick_in, place_in,
    out_any,
    c_ref, x1_ref, y1_ref, x2_ref, y2_ref, sig_ref, adj_ref, ay_ref, ax_ref, pick_ref, place_ref,
    out_ref, load_sem,
    tiles, mask_x, mask_y, ext, send_first, send_last, recv_first, recv_last,
    rows_low, rows_high, recv_low, recv_high,
    mapped, mapped_y2, state, edge, state_z,
    adj_ext, adj_edge, mid_ext, mid_edge,
    ax_send, ax_recv, ay_send, ay_recv, az_send, az_recv, gx_terms, gz_terms,
    send_sem, recv_sem,
):
    gx, gy, gz = lax.axis_index("gx"), lax.axis_index("gy"), lax.axis_index("gz")
    nx, ny = lax.axis_size("gx"), lax.axis_size("gy")
    x_up, x_down = {"gx": lax.rem(gx + 1, nx)}, {"gx": lax.rem(gx + nx - 1, nx)}
    y_up, y_down = {"gy": lax.rem(gy + 1, ny)}, {"gy": lax.rem(gy + ny - 1, ny)}
    z_other = {"gz": 1 - gz}
    barrier = pltpu.get_barrier_semaphore()
    for peer in (x_up, x_down, y_up, y_down, z_other):
        pl.semaphore_signal(barrier, inc=1, device_id=peer, device_id_type=MESH)

    pairs = (
        (sig_in, sig_ref), (x2_in, x2_ref), (y2_in, y2_ref), (c_in, c_ref), (x1_in, x1_ref),
        (y1_in, y1_ref), (pick_in, pick_ref), (adj_in, adj_ref), (place_in, place_ref),
        (ay_in, ay_ref), (ax_in, ax_ref),
    )
    loads = [
        pltpu.make_async_copy(source, target, load_sem.at[i])
        for i, (source, target) in enumerate(pairs)
    ]
    for load in loads:
        load.start()

    def remote(index, source, target, peer):
        return pltpu.make_async_remote_copy(
            src_ref=source,
            dst_ref=target,
            send_sem=send_sem.at[index],
            recv_sem=recv_sem.at[index],
            device_id=peer,
            device_id_type=MESH,
        )

    lane = lax.broadcasted_iota(jnp.int32, (8, 128), 1)
    lane_wide = lax.broadcasted_iota(jnp.int32, (32, 128), 1)

    for load in loads[:7]:
        load.wait()
    lane_tile = lax.broadcasted_iota(jnp.int32, (4, 64), 1) // 16
    row_half = lax.broadcasted_iota(jnp.int32, (8, 64), 0) < 4
    for c in range(2):
        for z in range(4):
            flags = sig_ref[c, z].astype(f32)
            wide = jnp.zeros((4, 64), f32)
            for t in range(4):
                wide = jnp.where(lane_tile == t, flags[:, t : t + 1], wide)
            tiles[c, z, 0:4] = wide
            each = [jnp.broadcast_to(tiles[c, z, t : t + 1], (8, 64)) for t in range(4)]
            for t in range(4):
                mask_y[c, z, 8 * t : 8 * t + 8] = each[t]
            for t in range(2):
                mask_x[c, z, 8 * t : 8 * t + 8] = jnp.where(row_half, each[2 * t], each[2 * t + 1])

    kept_x2 = x2_ref[...].astype(f32).reshape(2, 5, 4, 16, 64) * mask_x[...][:, None]
    kept_y2 = y2_ref[...].astype(f32).reshape(2, 5, 4, 32, 64) * mask_y[...][:, None]
    values = (
        c_ref[...],
        x1_ref[...],
        y1_ref[...],
        kept_x2.reshape(640, 64).astype(bf16),
        kept_y2.reshape(1280, 64).astype(bf16),
    )
    for (begin, end, width), value in zip(segments, values):
        pick = pick_ref[0 if width == 32 else 1][:, 0:width]
        ends = lax.dot_general(pick, value, (((1,), (1,)), ((), ())), preferred_element_type=f32)
        send_first[:, begin:end] = ends[0:8].astype(bf16)
        send_last[:, begin:end] = ends[8:16].astype(bf16)

    def pack_rims(source, which):
        for i in range(20):
            v, z = i // 4, i % 4
            ax_send[which, 0, i : i + 1] = source[v, z + 1, 8:9]
            ax_send[which, 1, i : i + 1] = source[v, z + 1, 39:40]
        first = jnp.zeros((32, 128), f32)
        last = jnp.zeros((32, 128), f32)
        for i in range(20):
            plane = source[i // 4, i % 4 + 1, 8:40]
            first = jnp.where(lane_wide == i, plane[:, 0:1], first)
            last = jnp.where(lane_wide == i, plane[:, 127:128], last)
        ay_send[which, 0] = first
        ay_send[which, 1] = last

    def rim_copies(source, which):
        base = 5 + 5 * which
        return [
            remote(base, ax_send.at[which, 0], ax_recv.at[which, 1], x_down),
            remote(base + 1, ax_send.at[which, 1], ax_recv.at[which, 0], x_up),
            remote(base + 2, ay_send.at[which, 0], ay_recv.at[which, 1], y_down),
            remote(base + 3, ay_send.at[which, 1], ay_recv.at[which, 0], y_up),
            remote(base + 4, source, az_recv.at[which], z_other),
        ]

    z_side = 3 - 3 * gz
    pl.semaphore_wait(barrier, 5)
    y_copies = [
        remote(0, send_first, recv_first, y_down),
        remote(1, send_last, recv_last, y_up),
    ]
    for copy in y_copies:
        copy.start()

    loads[7].wait()
    adj_ext[...] = jnp.zeros_like(adj_ext)
    for i in range(20):
        adj_ext[i // 4, i % 4 + 1, 8:40] = adj_ref[i // 4, i % 4]
    pack_rims(adj_ext, 0)
    adj_copies = rim_copies(adj_ref.at[:, z_side], 0)
    for copy in adj_copies:
        copy.start()

    ext[...] = jnp.zeros_like(ext)
    for (begin, end, width), value in zip(segments, values):
        ext[begin:end, 0:width] = value.astype(f32)
    mid_ext[...] = jnp.zeros_like(mid_ext)

    def fill_rims(target, target_edge, which):
        for i in range(20):
            v, z = i // 4, i % 4
            target[v, z + 1, 7:8] = ax_recv[which, 0, i : i + 1]
            target[v, z + 1, 40:41] = ax_recv[which, 1, i : i + 1]
            target_edge[v, z] = jnp.where(
                lane_wide == 0, ay_recv[which, 1, :, i : i + 1], ay_recv[which, 0, :, i : i + 1]
            )
        for v in range(5):
            plane = az_recv[which, v]
            target[v, 0, 8:40] = jnp.where(gz > 0, plane, 0.0)
            target[v, 5, 8:40] = jnp.where(gz > 0, 0.0, plane)

    for load in loads[8:]:
        load.wait()
    for copy in y_copies:
        copy.wait()
    joined = recv_first[...].astype(f32) + recv_last[...].astype(f32)
    ext[...] += jnp.dot(joined.T, place_ref[...], preferred_element_type=f32)

    coarse_e = ext[0:320].reshape(40, 8, 128)
    x1_e = ext[320:640].reshape(40, 8, 128)
    y1_e = ext[640:1280].reshape(40, 16, 128)
    x2_e = ext[1280:1920].reshape(40, 16, 128)
    y2_e = ext[1920:3200].reshape(40, 32, 128)
    blank = jnp.zeros((40, 1, 128), f32)
    low = jnp.concatenate(
        [coarse_e[:, 6:8], x1_e[:, 7:8], y1_e[:, 14:16], x2_e[:, 15:16], y2_e[:, 31:32], blank], 1
    )
    high = jnp.concatenate(
        [coarse_e[:, 0:3], x1_e[:, 0:1], y1_e[:, 0:2], y2_e[:, 0:1], blank], 1
    )
    rows_low[...] = low.reshape(320, 128).astype(bf16)
    rows_high[...] = high.reshape(320, 128).astype(bf16)
    x_copies = [
        remote(2, rows_low, recv_low, x_up),
        remote(3, rows_high, recv_high, x_down),
    ]
    for copy in x_copies:
        copy.start()

    for (begin, end, width), which, at in zip(segments, (0, 0, 1, 2, 3), (0, 8, 16, 32, None)):
        product = jnp.dot(
            ext[begin:end].astype(bf16), ay_ref[which], preferred_element_type=f32
        ).reshape(40, (end - begin) // 40, 256)
        if at is None:
            mapped_y2[...] = product
        else:
            mapped[:, at : at + (end - begin) // 40] = product

    for copy in adj_copies:
        copy.wait()
    fill_rims(adj_ext, adj_edge, 0)

    row_kind = lax.broadcasted_iota(jnp.int32, (320, 128), 0) % 8
    for copy in x_copies:
        copy.wait()
    for buffer, at, bounds in (
        (recv_low, 48, ((0, 3), (3, 5), (5, 6), (6, 8))),
        (recv_high, 56, ((0, 4), (4, 6), (6, 6), (6, 8))),
    ):
        received = buffer[...].astype(f32)
        total = jnp.zeros((320, 256), f32)
        for which, (begin, end) in enumerate(bounds):
            if begin < end:
                part = jnp.where((row_kind >= begin) & (row_kind < end), received, 0.0)
                total = total + jnp.dot(
                    part.astype(bf16), ay_ref[which], preferred_element_type=f32
                )
        mapped[:, at : at + 8] = total.reshape(40, 8, 256)

    def synthesize(order, cv, carry):
        for z in order:
            p = cv * 4 + z
            exact = mapped[p]
            coarse_bits = exact.astype(bf16)
            rest = (exact - coarse_bits.astype(f32)).astype(bf16)
            whole = jnp.dot(
                ax_ref[...],
                jnp.concatenate([coarse_bits, rest], axis=0),
                preferred_element_type=f32,
            )
            extra = mapped_y2[p]
            state[cv, z + 1, 0:8] = whole[0:8, 0:128]
            state[cv, z + 1, 8:40] = whole[8:40, 0:128] + extra[:, 0:128]
            state[cv, z + 1, 40:48] = whole[40:48, 0:128]
            edge[cv, z] = whole[8:40, 128:256] + extra[:, 128:256]
        return carry

    def synthesize_sides(pair, carry):
        for j in range(5):
            synthesize((z_side,), 5 * pair + j, carry)
        return carry

    lax.fori_loop(0, 2, synthesize_sides, 0)
    state_copy = remote(4, state.at[:, z_side + 1, 8:40], state_z, z_other)
    state_copy.start()
    lax.fori_loop(0, 10, functools.partial(synthesize, (gz, gz + 1, gz + 2)), 0)
    state_copy.wait()
    for cv in range(10):
        plane = state_z[cv]
        state[cv, 0, 8:40] = jnp.where(gz > 0, plane, 0.0)
        state[cv, 5, 8:40] = jnp.where(gz > 0, 0.0, plane)

    keep_bottom = jnp.where(gz > 0, 1.0, 0.0).astype(f32)

    def rate(base, source, source_edge, finish):
        def z_faces(k, carry):
            for r in range(4):
                at = slice(8 + 8 * r, 16 + 8 * r)
                mean = [0.5 * (state[base + v, k, at] + state[base + v, k + 1, at]) for v in range(5)]
                jump = [source[v, k + 1, at] - source[v, k, at] for v in range(5)]
                terms = face(mean, jump, 2)
                factor = jnp.where(k == 0, keep_bottom, 1.0)
                for v in range(5):
                    gz_terms[v, k, 8 * r : 8 * r + 8] = terms[v] * factor
            return carry

        lax.fori_loop(0, 5, z_faces, 0)

        def plane(z, carry):
            for r in range(5):
                low_at, high_at = slice(7 + 8 * r, 15 + 8 * r), slice(8 + 8 * r, 16 + 8 * r)
                mean = [
                    0.5 * (state[base + v, z + 1, low_at] + state[base + v, z + 1, high_at])
                    for v in range(5)
                ]
                jump = [source[v, z + 1, high_at] - source[v, z + 1, low_at] for v in range(5)]
                terms = face(mean, jump, 0)
                for v in range(5):
                    gx_terms[v, 8 * r : 8 * r + 8] = terms[v]
            for r in range(4):
                at, rows = slice(8 + 8 * r, 16 + 8 * r), slice(8 * r, 8 * r + 8)
                here = [state[base + v, z + 1, at] for v in range(5)]
                rim = [edge[base + v, z, rows] for v in range(5)]
                adj = [source[v, z + 1, at] for v in range(5)]
                adj_rim = [source_edge[v, z, rows] for v in range(5)]

                def ahead(a, b):
                    return pltpu.roll(jnp.where(lane == 0, b, a), 127, 1)

                def behind(a, b):
                    return pltpu.roll(jnp.where(lane == 127, b, a), 1, 1)

                adj_up = [ahead(adj[v], adj_rim[v]) for v in range(5)]
                adj_down = [behind(adj[v], adj_rim[v]) for v in range(5)]
                up = face(
                    [0.5 * (here[v] + ahead(here[v], rim[v])) for v in range(5)],
                    [adj_up[v] - adj[v] for v in range(5)],
                    1,
                )
                down = face(
                    [0.5 * (here[v] + behind(here[v], rim[v])) for v in range(5)],
                    [adj[v] - adj_down[v] for v in range(5)],
                    1,
                )
                for v in range(5):
                    halves = (
                        up[v]
                        + down[v]
                        + gx_terms[v, rows]
                        + gx_terms[v, 8 * r + 1 : 8 * r + 9]
                        + gz_terms[v, z, rows]
                        + gz_terms[v, z + 1, rows]
                    )
                    around = (
                        adj_up[v]
                        + adj_down[v]
                        + source[v, z + 1, 7 + 8 * r : 15 + 8 * r]
                        + source[v, z + 1, 9 + 8 * r : 17 + 8 * r]
                        + source[v, z, at]
                        + source[v, z + 2, at]
                    )
                    finish(v, z, rows, at, 0.5 * halves + viscosity * (around - 6.0 * adj[v]))
            return carry

        lax.fori_loop(0, 4, plane, 0)

    def finish_first(v, z, rows, at, value):
        held = adj_ext[v, z + 1, at]
        mid_ext[v, z + 1, at] = held + time_step * value
        out_ref[v, z, rows] = held + 0.5 * time_step * value

    def finish_second(v, z, rows, at, value):
        out_ref[v, z, rows] += 0.5 * time_step * value

    rate(0, adj_ext, adj_edge, finish_first)
    pack_rims(mid_ext, 1)
    mid_copies = rim_copies(mid_ext.at[:, z_side + 1, 8:40], 1)
    for copy in mid_copies:
        copy.start()
    for copy in mid_copies:
        copy.wait()
    fill_rims(mid_ext, mid_edge, 1)
    rate(5, mid_ext, mid_edge, finish_second)
    store = pltpu.make_async_copy(out_ref, out_any, load_sem.at[11])
    store.start()
    store.wait()


def shards(coarse, detail_x1, detail_y1, detail_x2, detail_y2, significance, adjoint):
    anywhere = pl.BlockSpec(memory_space=pl.ANY)
    return pl.pallas_call(
        kernel,
        out_shape=jax.ShapeDtypeStruct(adjoint.shape, f32),
        in_specs=[anywhere] * 11,
        out_specs=anywhere,
        scratch_shapes=[
            pltpu.VMEM((320, 32), bf16),
            pltpu.VMEM((320, 32), bf16),
            pltpu.VMEM((640, 32), bf16),
            pltpu.VMEM((640, 64), bf16),
            pltpu.VMEM((1280, 64), bf16),
            pltpu.VMEM((2, 4, 4, 4), jnp.int32),
            pltpu.VMEM((5, 4, 32, 128), f32),
            pltpu.VMEM((4, 128, 256), bf16),
            pltpu.VMEM((48, 128), bf16),
            pltpu.VMEM((2, 16, 64), bf16),
            pltpu.VMEM((8, 128), f32),
            pltpu.VMEM((5, 4, 32, 128), f32),
            pltpu.SemaphoreType.DMA((12,)),
            pltpu.VMEM((2, 4, 8, 64), f32),
            pltpu.VMEM((2, 4, 16, 64), f32),
            pltpu.VMEM((2, 4, 32, 64), f32),
            pltpu.VMEM((3200, 128), f32),
            pltpu.VMEM((8, 3200), bf16),
            pltpu.VMEM((8, 3200), bf16),
            pltpu.VMEM((8, 3200), bf16),
            pltpu.VMEM((8, 3200), bf16),
            pltpu.VMEM((320, 128), bf16),
            pltpu.VMEM((320, 128), bf16),
            pltpu.VMEM((320, 128), bf16),
            pltpu.VMEM((320, 128), bf16),
            pltpu.VMEM((40, 64, 256), f32),
            pltpu.VMEM((40, 32, 256), f32),
            pltpu.VMEM((10, 6, 48, 128), f32),
            pltpu.VMEM((10, 4, 32, 128), f32),
            pltpu.VMEM((10, 32, 128), f32),
            pltpu.VMEM((5, 6, 48, 128), f32),
            pltpu.VMEM((5, 4, 32, 128), f32),
            pltpu.VMEM((5, 6, 48, 128), f32),
            pltpu.VMEM((5, 4, 32, 128), f32),
            pltpu.VMEM((2, 2, 24, 128), f32),
            pltpu.VMEM((2, 2, 24, 128), f32),
            pltpu.VMEM((2, 2, 32, 128), f32),
            pltpu.VMEM((2, 2, 32, 128), f32),
            pltpu.VMEM((8, 128), f32),
            pltpu.VMEM((2, 5, 32, 128), f32),
            pltpu.VMEM((5, 40, 128), f32),
            pltpu.VMEM((5, 5, 32, 128), f32),
            pltpu.SemaphoreType.DMA((15,)),
            pltpu.SemaphoreType.DMA((15,)),
        ],
        compiler_params=pltpu.CompilerParams(collective_id=0, has_side_effects=True),
    )(
        coarse.reshape(320, 32),
        detail_x1.reshape(320, 32),
        detail_y1.reshape(640, 32),
        detail_x2.reshape(640, 64),
        detail_y2.reshape(1280, 64),
        significance,
        adjoint,
        jnp.asarray(y_matrices()),
        jnp.asarray(x_matrix()),
        jnp.asarray(pick_matrices()),
        jnp.asarray(place_matrix()),
    )


def solution(mesh):
    return jax.shard_map(
        shards,
        mesh=mesh,
        in_specs=(
            P(None, None, "gz", "gx", "gy"),
            P(None, None, "gz", "gx", "gy"),
            P(None, None, "gz", "gx", "gy"),
            P(None, None, "gz", "gx", "gy"),
            P(None, None, "gz", "gx", "gy"),
            P(None, "gz", "gx", "gy"),
            P(None, "gz", "gx", "gy"),
        ),
        out_specs=P(None, "gz", "gx", "gy"),
        check_vma=False,
    )
```

```python
import functools

import jax
import jax.numpy as jnp
import ml_dtypes
import numpy as np
from jax import lax
from jax.experimental import pallas as pl
from jax.experimental.pallas import tpu as pltpu
from jax.sharding import PartitionSpec as P

time_step = 0.1
viscosity = 0.2
heat_ratio_less_one = 0.4
f32 = jnp.float32
bf16 = jnp.bfloat16
MESH = pl.DeviceIdType.MESH
segments = ((0, 320, 32), (320, 640, 32), (640, 1280, 32), (1280, 1920, 64), (1920, 3200, 64))


def predict(index):
    k = index // 2
    if index % 2 == 0:
        return {("c", k): 1.0}
    return {
        ("d", k): 1.0,
        ("c", k): 9 / 16,
        ("c", k + 1): 9 / 16,
        ("c", k - 1): -1 / 16,
        ("c", k + 2): -1 / 16,
    }


def predict_twice(index):
    whole = {}
    for (kind, k), weight in predict(index).items():
        if kind == "d":
            whole[("e", k)] = weight
            continue
        whole[("m", k)] = weight
        for key, inner in predict(k).items():
            whole[key] = whole.get(key, 0.0) + weight * inner
    return whole


def lane_of(k, length):
    if k < 0:
        return 69 + k
    return k if k < length else 64 + k - length


def y_matrices():
    mats = np.zeros((4, 128, 256), np.float32)
    columns = [(y, y) for y in range(128)] + [(128, 128), (-1, 255)]
    for y, column in columns:
        for (kind, k), weight in predict_twice(y).items():
            which = "cdme".index(kind)
            mats[which, lane_of(k, 32 if which < 2 else 64), column] += weight
    return mats.astype(ml_dtypes.bfloat16)


def x_matrix():
    mat = np.zeros((48, 64), np.float32)
    for x in range(-1, 33):
        row = x + 8
        for (kind, k), weight in predict_twice(x).items():
            if kind == "c":
                at = 50 + k if k < 0 else (k if k < 8 else 56 + k - 8)
            elif kind == "d":
                at = 50 if k < 0 else (8 + k if k < 8 else 59)
            elif kind == "m":
                at = 53 + k if k < 0 else (16 + k if k < 16 else 60 + k - 16)
            else:
                at = 53 if k < 0 else 32 + k
            mat[row, at] += weight
    mat[7, 54] = 1.0
    mat[40, 62] = 1.0
    return np.concatenate([mat, mat], axis=1).astype(ml_dtypes.bfloat16)


def pick_matrices():
    pick = np.zeros((2, 16, 64), np.float32)
    for which, width in ((0, 32), (1, 64)):
        for j in range(3):
            pick[which, j, j] = 1.0
        pick[which, 11, width - 2] = 1.0
        pick[which, 12, width - 1] = 1.0
    return pick.astype(ml_dtypes.bfloat16)


def place_matrix():
    place = np.zeros((8, 128), np.float32)
    for j in range(5):
        place[j, 64 + j] = 1.0
    return place


def face(mean, jump, k):
    q, u, t = mean[0], mean[1:4], mean[4]
    rho = jnp.exp(0.5 * q)
    speed = u[k]
    half_square = 0.5 * (u[0] * u[0] + u[1] * u[1] + u[2] * u[2])
    enthalpy = (1.0 / heat_ratio_less_one + 1.0) * t + half_square
    inner = jump[0] + jump[1] * u[0] + jump[2] * u[1] + jump[3] * u[2] + jump[4] * enthalpy
    flow = rho * speed
    grads = [flow * (jump[1 + j] + jump[4] * u[j]) for j in range(3)]
    grads[k] = grads[k] + rho * inner
    dq = 0.5 * (flow * inner + rho * t * jump[1 + k])
    dt = rho * jump[1 + k] + (1.0 / heat_ratio_less_one + 1.0) * flow * jump[4]
    return [dq] + grads + [dt]


def kernel(
    c_in, x1_in, y1_in, x2_in, y2_in, sig_in, adj_in, ay_in, ax_in, pick_in, place_in,
    out_any,
    c_ref, x1_ref, y1_ref, x2_ref, y2_ref, sig_ref, adj_ref, ay_ref, ax_ref, pick_ref, place_ref,
    out_ref, load_sem,
    tiles, mask_x, mask_y, ext, send_first, send_last, recv_first, recv_last,
    rows_low, rows_high, recv_low, recv_high,
    mapped, mapped_y2, state, edge, state_z,
    adj_ext, adj_edge, mid_ext, mid_edge,
    ax_send, ax_recv, ay_send, ay_recv, az_recv, gx_terms, gy_terms, gz_terms,
    send_sem, recv_sem,
):
    gx, gy, gz = lax.axis_index("gx"), lax.axis_index("gy"), lax.axis_index("gz")
    nx, ny = lax.axis_size("gx"), lax.axis_size("gy")
    x_up, x_down = {"gx": lax.rem(gx + 1, nx)}, {"gx": lax.rem(gx + nx - 1, nx)}
    y_up, y_down = {"gy": lax.rem(gy + 1, ny)}, {"gy": lax.rem(gy + ny - 1, ny)}
    z_other = {"gz": 1 - gz}
    barrier = pltpu.get_barrier_semaphore()
    for peer in (x_up, x_down, y_up, y_down, z_other):
        pl.semaphore_signal(barrier, inc=1, device_id=peer, device_id_type=MESH)

    pairs = (
        (sig_in, sig_ref), (x2_in, x2_ref), (y2_in, y2_ref), (c_in, c_ref), (x1_in, x1_ref),
        (y1_in, y1_ref), (pick_in, pick_ref), (adj_in, adj_ref), (place_in, place_ref),
        (ay_in, ay_ref), (ax_in, ax_ref),
    )
    loads = [
        pltpu.make_async_copy(source, target, load_sem.at[i])
        for i, (source, target) in enumerate(pairs)
    ]
    for load in loads:
        load.start()

    def remote(index, source, target, peer):
        return pltpu.make_async_remote_copy(
            src_ref=source,
            dst_ref=target,
            send_sem=send_sem.at[index],
            recv_sem=recv_sem.at[index],
            device_id=peer,
            device_id_type=MESH,
        )

    lane = lax.broadcasted_iota(jnp.int32, (8, 128), 1)
    lane_wide = lax.broadcasted_iota(jnp.int32, (32, 128), 1)

    for load in loads[:7]:
        load.wait()
    lane_tile = lax.broadcasted_iota(jnp.int32, (4, 64), 1) // 16
    row_half = lax.broadcasted_iota(jnp.int32, (8, 64), 0) < 4
    for c in range(2):
        for z in range(4):
            flags = sig_ref[c, z].astype(f32)
            wide = jnp.zeros((4, 64), f32)
            for t in range(4):
                wide = jnp.where(lane_tile == t, flags[:, t : t + 1], wide)
            tiles[c, z, 0:4] = wide
            each = [jnp.broadcast_to(tiles[c, z, t : t + 1], (8, 64)) for t in range(4)]
            for t in range(4):
                mask_y[c, z, 8 * t : 8 * t + 8] = each[t]
            for t in range(2):
                mask_x[c, z, 8 * t : 8 * t + 8] = jnp.where(row_half, each[2 * t], each[2 * t + 1])

    kept_x2 = x2_ref[...].astype(f32).reshape(2, 5, 4, 16, 64) * mask_x[...][:, None]
    kept_y2 = y2_ref[...].astype(f32).reshape(2, 5, 4, 32, 64) * mask_y[...][:, None]
    values = (
        c_ref[...],
        x1_ref[...],
        y1_ref[...],
        kept_x2.reshape(640, 64).astype(bf16),
        kept_y2.reshape(1280, 64).astype(bf16),
    )
    for (begin, end, width), value in zip(segments, values):
        pick = pick_ref[0 if width == 32 else 1][:, 0:width]
        ends = lax.dot_general(pick, value, (((1,), (1,)), ((), ())), preferred_element_type=f32)
        send_first[:, begin:end] = ends[0:8].astype(bf16)
        send_last[:, begin:end] = ends[8:16].astype(bf16)

    def pack_rims(source, which):
        for i in range(20):
            v, z = i // 4, i % 4
            ax_send[which, 0, i : i + 1] = source[v, z + 1, 8:9]
            ax_send[which, 1, i : i + 1] = source[v, z + 1, 39:40]
        first = jnp.zeros((32, 128), f32)
        last = jnp.zeros((32, 128), f32)
        for i in range(20):
            plane = source[i // 4, i % 4 + 1, 8:40]
            first = jnp.where(lane_wide == i, plane[:, 0:1], first)
            last = jnp.where(lane_wide == i, plane[:, 127:128], last)
        ay_send[which, 0] = first
        ay_send[which, 1] = last

    def rim_copies(source, which):
        base = 5 + 5 * which
        return [
            remote(base, ax_send.at[which, 0], ax_recv.at[which, 1], x_down),
            remote(base + 1, ax_send.at[which, 1], ax_recv.at[which, 0], x_up),
            remote(base + 2, ay_send.at[which, 0], ay_recv.at[which, 1], y_down),
            remote(base + 3, ay_send.at[which, 1], ay_recv.at[which, 0], y_up),
            remote(base + 4, source, az_recv.at[which], z_other),
        ]

    z_side = 3 - 3 * gz
    pl.semaphore_wait(barrier, 5)
    y_copies = [
        remote(0, send_first, recv_first, y_down),
        remote(1, send_last, recv_last, y_up),
    ]
    for copy in y_copies:
        copy.start()

    loads[7].wait()
    adj_ext[...] = jnp.zeros_like(adj_ext)
    for i in range(20):
        adj_ext[i // 4, i % 4 + 1, 8:40] = adj_ref[i // 4, i % 4]
    pack_rims(adj_ext, 0)
    adj_copies = rim_copies(adj_ref.at[:, z_side], 0)
    for copy in adj_copies:
        copy.start()

    ext[...] = jnp.zeros_like(ext)
    for (begin, end, width), value in zip(segments, values):
        ext[begin:end, 0:width] = value.astype(f32)
    mid_ext[...] = jnp.zeros_like(mid_ext)

    def fill_rims(target, target_edge, which):
        for i in range(20):
            v, z = i // 4, i % 4
            target[v, z + 1, 7:8] = ax_recv[which, 0, i : i + 1]
            target[v, z + 1, 40:41] = ax_recv[which, 1, i : i + 1]
            target_edge[v, z] = jnp.where(
                lane_wide == 0, ay_recv[which, 1, :, i : i + 1], ay_recv[which, 0, :, i : i + 1]
            )
        for v in range(5):
            plane = az_recv[which, v]
            target[v, 0, 8:40] = jnp.where(gz > 0, plane, 0.0)
            target[v, 5, 8:40] = jnp.where(gz > 0, 0.0, plane)

    for load in loads[8:]:
        load.wait()
    for copy in y_copies:
        copy.wait()
    joined = recv_first[...].astype(f32) + recv_last[...].astype(f32)
    ext[...] += jnp.dot(joined.T, place_ref[...], preferred_element_type=f32)

    coarse_e = ext[0:320].reshape(40, 8, 128)
    x1_e = ext[320:640].reshape(40, 8, 128)
    y1_e = ext[640:1280].reshape(40, 16, 128)
    x2_e = ext[1280:1920].reshape(40, 16, 128)
    y2_e = ext[1920:3200].reshape(40, 32, 128)
    blank = jnp.zeros((40, 1, 128), f32)
    low = jnp.concatenate(
        [coarse_e[:, 6:8], x1_e[:, 7:8], y1_e[:, 14:16], x2_e[:, 15:16], y2_e[:, 31:32], blank], 1
    )
    high = jnp.concatenate(
        [coarse_e[:, 0:3], x1_e[:, 0:1], y1_e[:, 0:2], y2_e[:, 0:1], blank], 1
    )
    rows_low[...] = low.reshape(320, 128).astype(bf16)
    rows_high[...] = high.reshape(320, 128).astype(bf16)
    x_copies = [
        remote(2, rows_low, recv_low, x_up),
        remote(3, rows_high, recv_high, x_down),
    ]
    for copy in x_copies:
        copy.start()

    for (begin, end, width), which, at in zip(segments, (0, 0, 1, 2, 3), (0, 8, 16, 32, None)):
        product = jnp.dot(
            ext[begin:end].astype(bf16), ay_ref[which], preferred_element_type=f32
        ).reshape(40, (end - begin) // 40, 256)
        if at is None:
            mapped_y2[...] = product
        else:
            mapped[:, at : at + (end - begin) // 40] = product

    for copy in adj_copies:
        copy.wait()
    fill_rims(adj_ext, adj_edge, 0)

    row_kind = lax.broadcasted_iota(jnp.int32, (320, 128), 0) % 8
    for copy in x_copies:
        copy.wait()
    for buffer, at, bounds in (
        (recv_low, 48, ((0, 3), (3, 5), (5, 6), (6, 8))),
        (recv_high, 56, ((0, 4), (4, 6), (6, 6), (6, 8))),
    ):
        received = buffer[...].astype(f32)
        total = jnp.zeros((320, 256), f32)
        for which, (begin, end) in enumerate(bounds):
            if begin < end:
                part = jnp.where((row_kind >= begin) & (row_kind < end), received, 0.0)
                total = total + jnp.dot(
                    part.astype(bf16), ay_ref[which], preferred_element_type=f32
                )
        mapped[:, at : at + 8] = total.reshape(40, 8, 256)

    def synthesize(order, cv, carry):
        for z in order:
            p = cv * 4 + z
            exact = mapped[p]
            coarse_bits = exact.astype(bf16)
            rest = (exact - coarse_bits.astype(f32)).astype(bf16)
            whole = jnp.dot(
                ax_ref[...],
                jnp.concatenate([coarse_bits, rest], axis=0),
                preferred_element_type=f32,
            )
            extra = mapped_y2[p]
            state[cv, z + 1, 0:8] = whole[0:8, 0:128]
            state[cv, z + 1, 8:40] = whole[8:40, 0:128] + extra[:, 0:128]
            state[cv, z + 1, 40:48] = whole[40:48, 0:128]
            edge[cv, z] = whole[8:40, 128:256] + extra[:, 128:256]
        return carry

    def synthesize_sides(pair, carry):
        for j in range(5):
            synthesize((z_side,), 5 * pair + j, carry)
        return carry

    keep_bottom = jnp.where(gz > 0, 1.0, 0.0).astype(f32)

    def z_faces(base, source, k):
        for r in range(4):
            at = slice(8 + 8 * r, 16 + 8 * r)
            mean = [0.5 * (state[base + v, k, at] + state[base + v, k + 1, at]) for v in range(5)]
            jump = [source[v, k + 1, at] - source[v, k, at] for v in range(5)]
            terms = face(mean, jump, 2)
            for v in range(5):
                gz_terms[v, k, 8 * r : 8 * r + 8] = terms[v]

    def x_faces(base, source, z, r):
        low_at, high_at = slice(7 + 8 * r, 15 + 8 * r), slice(8 + 8 * r, 16 + 8 * r)
        mean = [
            0.5 * (state[base + v, z + 1, low_at] + state[base + v, z + 1, high_at])
            for v in range(5)
        ]
        jump = [source[v, z + 1, high_at] - source[v, z + 1, low_at] for v in range(5)]
        terms = face(mean, jump, 0)
        for v in range(5):
            gx_terms[z, v, 8 * r : 8 * r + 8] = terms[v]

    def inner_faces(base, source):
        def middle_z(k, carry):
            z_faces(base, source, k)
            return carry

        lax.fori_loop(1, 4, middle_z, 0)

        def plane(z, carry):
            for r in range(1, 4):
                x_faces(base, source, z, r)
            for r in range(4):
                at, rows = slice(8 + 8 * r, 16 + 8 * r), slice(8 * r, 8 * r + 8)
                here = [state[base + v, z + 1, at] for v in range(5)]
                adj = [source[v, z + 1, at] for v in range(5)]
                terms = face(
                    [0.5 * (a + pltpu.roll(a, 127, 1)) for a in here],
                    [pltpu.roll(a, 127, 1) - a for a in adj],
                    1,
                )
                for v in range(5):
                    gy_terms[z, v, rows] = terms[v]
            return carry

        lax.fori_loop(0, 4, plane, 0)

    def rate(base, source, source_edge, finish):
        z_faces(base, source, 0)
        gz_terms[:, 0] = gz_terms[:, 0] * keep_bottom
        z_faces(base, source, 4)

        def plane(z, carry):
            x_faces(base, source, z, 0)
            x_faces(base, source, z, 4)
            for r in range(4):
                at, rows = slice(8 + 8 * r, 16 + 8 * r), slice(8 * r, 8 * r + 8)
                rim = [edge[base + v, z, rows] for v in range(5)]
                adj = [source[v, z + 1, at] for v in range(5)]
                adj_rim = [source_edge[v, z, rows] for v in range(5)]

                def across(a):
                    return jnp.where(lane == 0, pltpu.roll(a, 1, 1), pltpu.roll(a, 127, 1))

                jump = [adj_rim[v] - across(adj[v]) for v in range(5)]
                terms = face(
                    [0.5 * (rim[v] + across(state[base + v, z + 1, at])) for v in range(5)],
                    [jnp.where(lane == 0, gap, -gap) for gap in jump],
                    1,
                )
                for v in range(5):
                    held = gy_terms[z, v, rows]
                    up = jnp.where(lane == 127, pltpu.roll(terms[v], 127, 1), held)
                    down = pltpu.roll(jnp.where(lane == 127, terms[v], held), 1, 1)
                    halves = (
                        up
                        + down
                        + gx_terms[z, v, rows]
                        + gx_terms[z, v, 8 * r + 1 : 8 * r + 9]
                        + gz_terms[v, z, rows]
                        + gz_terms[v, z + 1, rows]
                    )
                    around = (
                        pltpu.roll(jnp.where(lane == 0, adj_rim[v], adj[v]), 127, 1)
                        + pltpu.roll(jnp.where(lane == 127, adj_rim[v], adj[v]), 1, 1)
                        + source[v, z + 1, 7 + 8 * r : 15 + 8 * r]
                        + source[v, z + 1, 9 + 8 * r : 17 + 8 * r]
                        + source[v, z, at]
                        + source[v, z + 2, at]
                    )
                    finish(v, z, rows, at, 0.5 * halves + viscosity * (around - 6.0 * adj[v]))
            return carry

        lax.fori_loop(0, 4, plane, 0)

    lax.fori_loop(0, 2, synthesize_sides, 0)
    state_copy = remote(4, state.at[:, z_side + 1, 8:40], state_z, z_other)
    state_copy.start()
    lax.fori_loop(0, 10, functools.partial(synthesize, (gz, gz + 1, gz + 2)), 0)
    inner_faces(0, adj_ext)
    state_copy.wait()
    for cv in range(10):
        plane = state_z[cv]
        state[cv, 0, 8:40] = jnp.where(gz > 0, plane, 0.0)
        state[cv, 5, 8:40] = jnp.where(gz > 0, 0.0, plane)

    def finish_first(v, z, rows, at, value):
        held = adj_ext[v, z + 1, at]
        mid_ext[v, z + 1, at] = held + time_step * value
        out_ref[v, z, rows] = held + 0.5 * time_step * value

    def finish_second(v, z, rows, at, value):
        out_ref[v, z, rows] += 0.5 * time_step * value

    rate(0, adj_ext, adj_edge, finish_first)
    mid_copies = rim_copies(mid_ext.at[:, z_side + 1, 8:40], 1)
    pack_rims(mid_ext, 1)
    for copy in mid_copies[2:4] + mid_copies[0:2] + mid_copies[4:5]:
        copy.start()
    inner_faces(5, mid_ext)
    for copy in mid_copies:
        copy.wait()
    fill_rims(mid_ext, mid_edge, 1)
    rate(5, mid_ext, mid_edge, finish_second)
    store = pltpu.make_async_copy(out_ref, out_any, load_sem.at[11])
    store.start()
    store.wait()


def shards(coarse, detail_x1, detail_y1, detail_x2, detail_y2, significance, adjoint):
    anywhere = pl.BlockSpec(memory_space=pl.ANY)
    return pl.pallas_call(
        kernel,
        out_shape=jax.ShapeDtypeStruct(adjoint.shape, f32),
        in_specs=[anywhere] * 11,
        out_specs=anywhere,
        scratch_shapes=[
            pltpu.VMEM((320, 32), bf16),
            pltpu.VMEM((320, 32), bf16),
            pltpu.VMEM((640, 32), bf16),
            pltpu.VMEM((640, 64), bf16),
            pltpu.VMEM((1280, 64), bf16),
            pltpu.VMEM((2, 4, 4, 4), jnp.int32),
            pltpu.VMEM((5, 4, 32, 128), f32),
            pltpu.VMEM((4, 128, 256), bf16),
            pltpu.VMEM((48, 128), bf16),
            pltpu.VMEM((2, 16, 64), bf16),
            pltpu.VMEM((8, 128), f32),
            pltpu.VMEM((5, 4, 32, 128), f32),
            pltpu.SemaphoreType.DMA((12,)),
            pltpu.VMEM((2, 4, 8, 64), f32),
            pltpu.VMEM((2, 4, 16, 64), f32),
            pltpu.VMEM((2, 4, 32, 64), f32),
            pltpu.VMEM((3200, 128), f32),
            pltpu.VMEM((8, 3200), bf16),
            pltpu.VMEM((8, 3200), bf16),
            pltpu.VMEM((8, 3200), bf16),
            pltpu.VMEM((8, 3200), bf16),
            pltpu.VMEM((320, 128), bf16),
            pltpu.VMEM((320, 128), bf16),
            pltpu.VMEM((320, 128), bf16),
            pltpu.VMEM((320, 128), bf16),
            pltpu.VMEM((40, 64, 256), f32),
            pltpu.VMEM((40, 32, 256), f32),
            pltpu.VMEM((10, 6, 48, 128), f32),
            pltpu.VMEM((10, 4, 32, 128), f32),
            pltpu.VMEM((10, 32, 128), f32),
            pltpu.VMEM((5, 6, 48, 128), f32),
            pltpu.VMEM((5, 4, 32, 128), f32),
            pltpu.VMEM((5, 6, 48, 128), f32),
            pltpu.VMEM((5, 4, 32, 128), f32),
            pltpu.VMEM((2, 2, 24, 128), f32),
            pltpu.VMEM((2, 2, 24, 128), f32),
            pltpu.VMEM((2, 2, 32, 128), f32),
            pltpu.VMEM((2, 2, 32, 128), f32),
            pltpu.VMEM((2, 5, 32, 128), f32),
            pltpu.VMEM((4, 5, 40, 128), f32),
            pltpu.VMEM((4, 5, 32, 128), f32),
            pltpu.VMEM((5, 5, 32, 128), f32),
            pltpu.SemaphoreType.DMA((15,)),
            pltpu.SemaphoreType.DMA((15,)),
        ],
        compiler_params=pltpu.CompilerParams(collective_id=0, has_side_effects=True),
    )(
        coarse.reshape(320, 32),
        detail_x1.reshape(320, 32),
        detail_y1.reshape(640, 32),
        detail_x2.reshape(640, 64),
        detail_y2.reshape(1280, 64),
        significance,
        adjoint,
        jnp.asarray(y_matrices()),
        jnp.asarray(x_matrix()),
        jnp.asarray(pick_matrices()),
        jnp.asarray(place_matrix()),
    )


def solution(mesh):
    return jax.shard_map(
        shards,
        mesh=mesh,
        in_specs=(
            P(None, None, "gz", "gx", "gy"),
            P(None, None, "gz", "gx", "gy"),
            P(None, None, "gz", "gx", "gy"),
            P(None, None, "gz", "gx", "gy"),
            P(None, None, "gz", "gx", "gy"),
            P(None, "gz", "gx", "gy"),
            P(None, "gz", "gx", "gy"),
        ),
        out_specs=P(None, "gz", "gx", "gy"),
        check_vma=False,
    )
```

```python
import functools

import jax
import jax.numpy as jnp
import ml_dtypes
import numpy as np
from jax import lax
from jax.experimental import pallas as pl
from jax.experimental.pallas import tpu as pltpu
from jax.sharding import PartitionSpec as P

time_step = 0.1
viscosity = 0.2
heat_ratio_less_one = 0.4
f32 = jnp.float32
bf16 = jnp.bfloat16
MESH = pl.DeviceIdType.MESH
segments = ((0, 320, 32), (320, 640, 32), (640, 1280, 32), (1280, 1920, 64), (1920, 3200, 64))


def predict(index):
    k = index // 2
    if index % 2 == 0:
        return {("c", k): 1.0}
    return {
        ("d", k): 1.0,
        ("c", k): 9 / 16,
        ("c", k + 1): 9 / 16,
        ("c", k - 1): -1 / 16,
        ("c", k + 2): -1 / 16,
    }


def predict_twice(index):
    whole = {}
    for (kind, k), weight in predict(index).items():
        if kind == "d":
            whole[("e", k)] = weight
            continue
        whole[("m", k)] = weight
        for key, inner in predict(k).items():
            whole[key] = whole.get(key, 0.0) + weight * inner
    return whole


def lane_of(k, length):
    if k < 0:
        return 69 + k
    return k if k < length else 64 + k - length


def y_matrices():
    mats = np.zeros((4, 128, 256), np.float32)
    columns = [(y, y) for y in range(128)] + [(128, 128), (-1, 255)]
    for y, column in columns:
        for (kind, k), weight in predict_twice(y).items():
            which = "cdme".index(kind)
            mats[which, lane_of(k, 32 if which < 2 else 64), column] += weight
    return mats.astype(ml_dtypes.bfloat16)


def x_matrix():
    mat = np.zeros((48, 64), np.float32)
    for x in range(-1, 33):
        row = x + 8
        for (kind, k), weight in predict_twice(x).items():
            if kind == "c":
                at = 50 + k if k < 0 else (k if k < 8 else 56 + k - 8)
            elif kind == "d":
                at = 50 if k < 0 else (8 + k if k < 8 else 59)
            elif kind == "m":
                at = 53 + k if k < 0 else (16 + k if k < 16 else 60 + k - 16)
            else:
                at = 53 if k < 0 else 32 + k
            mat[row, at] += weight
    mat[7, 54] = 1.0
    mat[40, 62] = 1.0
    return np.concatenate([mat, mat], axis=1).astype(ml_dtypes.bfloat16)


def pick_matrices():
    pick = np.zeros((2, 16, 64), np.float32)
    for which, width in ((0, 32), (1, 64)):
        for j in range(3):
            pick[which, j, j] = 1.0
        pick[which, 11, width - 2] = 1.0
        pick[which, 12, width - 1] = 1.0
    return pick.astype(ml_dtypes.bfloat16)


def place_matrix():
    place = np.zeros((8, 128), np.float32)
    for j in range(5):
        place[j, 64 + j] = 1.0
    return place


def face(mean, jump, k):
    q, u, t = mean[0], mean[1:4], mean[4]
    rho = jnp.exp(0.5 * q)
    speed = u[k]
    half_square = 0.5 * (u[0] * u[0] + u[1] * u[1] + u[2] * u[2])
    enthalpy = (1.0 / heat_ratio_less_one + 1.0) * t + half_square
    inner = jump[0] + jump[1] * u[0] + jump[2] * u[1] + jump[3] * u[2] + jump[4] * enthalpy
    flow = rho * speed
    grads = [flow * (jump[1 + j] + jump[4] * u[j]) for j in range(3)]
    grads[k] = grads[k] + rho * inner
    dq = 0.5 * (flow * inner + rho * t * jump[1 + k])
    dt = rho * jump[1 + k] + (1.0 / heat_ratio_less_one + 1.0) * flow * jump[4]
    return [dq] + grads + [dt]


def kernel(
    c_in, x1_in, y1_in, x2_in, y2_in, sig_in, adj_in, ay_in, ax_in, pick_in, place_in,
    out_any,
    c_ref, x1_ref, y1_ref, x2_ref, y2_ref, sig_ref, adj_ref, ay_ref, ax_ref, pick_ref, place_ref,
    out_ref, load_sem,
    tiles, mask_x, mask_y, ext, send_first, send_last, recv_first, recv_last,
    rows_low, rows_high, recv_low, recv_high,
    mapped, mapped_y2, state, edge, state_z,
    adj_ext, adj_edge, mid_ext, mid_edge,
    ax_send, ax_recv, ay_send, ay_recv, az_send, az_recv, gx_terms, gz_terms,
    send_sem, recv_sem,
):
    gx, gy, gz = lax.axis_index("gx"), lax.axis_index("gy"), lax.axis_index("gz")
    nx, ny = lax.axis_size("gx"), lax.axis_size("gy")
    x_up, x_down = {"gx": lax.rem(gx + 1, nx)}, {"gx": lax.rem(gx + nx - 1, nx)}
    y_up, y_down = {"gy": lax.rem(gy + 1, ny)}, {"gy": lax.rem(gy + ny - 1, ny)}
    z_other = {"gz": 1 - gz}
    barrier = pltpu.get_barrier_semaphore()
    for peer in (x_up, x_down, y_up, y_down, z_other):
        pl.semaphore_signal(barrier, inc=1, device_id=peer, device_id_type=MESH)

    pairs = (
        (sig_in, sig_ref), (x2_in, x2_ref), (y2_in, y2_ref), (c_in, c_ref), (x1_in, x1_ref),
        (y1_in, y1_ref), (pick_in, pick_ref), (adj_in, adj_ref), (place_in, place_ref),
        (ay_in, ay_ref), (ax_in, ax_ref),
    )
    loads = [
        pltpu.make_async_copy(source, target, load_sem.at[i])
        for i, (source, target) in enumerate(pairs)
    ]
    for load in loads:
        load.start()

    def remote(index, source, target, peer):
        return pltpu.make_async_remote_copy(
            src_ref=source,
            dst_ref=target,
            send_sem=send_sem.at[index],
            recv_sem=recv_sem.at[index],
            device_id=peer,
            device_id_type=MESH,
        )

    lane = lax.broadcasted_iota(jnp.int32, (8, 128), 1)
    lane_wide = lax.broadcasted_iota(jnp.int32, (32, 128), 1)

    for load in loads[:7]:
        load.wait()
    lane_tile = lax.broadcasted_iota(jnp.int32, (4, 64), 1) // 16
    row_half = lax.broadcasted_iota(jnp.int32, (8, 64), 0) < 4
    for c in range(2):
        for z in range(4):
            flags = sig_ref[c, z].astype(f32)
            wide = jnp.zeros((4, 64), f32)
            for t in range(4):
                wide = jnp.where(lane_tile == t, flags[:, t : t + 1], wide)
            tiles[c, z, 0:4] = wide
            each = [jnp.broadcast_to(tiles[c, z, t : t + 1], (8, 64)) for t in range(4)]
            for t in range(4):
                mask_y[c, z, 8 * t : 8 * t + 8] = each[t]
            for t in range(2):
                mask_x[c, z, 8 * t : 8 * t + 8] = jnp.where(row_half, each[2 * t], each[2 * t + 1])

    kept_x2 = x2_ref[...].astype(f32).reshape(2, 5, 4, 16, 64) * mask_x[...][:, None]
    kept_y2 = y2_ref[...].astype(f32).reshape(2, 5, 4, 32, 64) * mask_y[...][:, None]
    values = (
        c_ref[...],
        x1_ref[...],
        y1_ref[...],
        kept_x2.reshape(640, 64).astype(bf16),
        kept_y2.reshape(1280, 64).astype(bf16),
    )
    for (begin, end, width), value in zip(segments, values):
        pick = pick_ref[0 if width == 32 else 1][:, 0:width]
        ends = lax.dot_general(pick, value, (((1,), (1,)), ((), ())), preferred_element_type=f32)
        send_first[:, begin:end] = ends[0:8].astype(bf16)
        send_last[:, begin:end] = ends[8:16].astype(bf16)

    def pack_rows(source, which):
        for i in range(20):
            v, z = i // 4, i % 4
            ax_send[which, 0, i : i + 1] = source[v, z + 1, 8:9]
            ax_send[which, 1, i : i + 1] = source[v, z + 1, 39:40]

    def pack_columns(source, which):
        first = jnp.zeros((32, 128), f32)
        last = jnp.zeros((32, 128), f32)
        for i in range(20):
            plane = source[i // 4, i % 4 + 1, 8:40]
            first = jnp.where(lane_wide == i, plane[:, 0:1], first)
            last = jnp.where(lane_wide == i, plane[:, 127:128], last)
        ay_send[which, 0] = first
        ay_send[which, 1] = last

    def rim_copies(source, which):
        base = 5 + 5 * which
        return [
            remote(base, ax_send.at[which, 0], ax_recv.at[which, 1], x_down),
            remote(base + 1, ax_send.at[which, 1], ax_recv.at[which, 0], x_up),
            remote(base + 2, ay_send.at[which, 0], ay_recv.at[which, 1], y_down),
            remote(base + 3, ay_send.at[which, 1], ay_recv.at[which, 0], y_up),
            remote(base + 4, source, az_recv.at[which], z_other),
        ]

    z_side = 3 - 3 * gz
    pl.semaphore_wait(barrier, 5)
    y_copies = [
        remote(0, send_first, recv_first, y_down),
        remote(1, send_last, recv_last, y_up),
    ]
    for copy in y_copies:
        copy.start()

    loads[7].wait()
    adj_ext[...] = jnp.zeros_like(adj_ext)
    for i in range(20):
        adj_ext[i // 4, i % 4 + 1, 8:40] = adj_ref[i // 4, i % 4]
    pack_rows(adj_ext, 0)
    pack_columns(adj_ext, 0)
    adj_copies = rim_copies(adj_ref.at[:, z_side], 0)
    for copy in adj_copies:
        copy.start()

    ext[...] = jnp.zeros_like(ext)
    for (begin, end, width), value in zip(segments, values):
        ext[begin:end, 0:width] = value.astype(f32)
    mid_ext[...] = jnp.zeros_like(mid_ext)

    def fill_columns(target_edge, which):
        for i in range(20):
            target_edge[i // 4, i % 4] = jnp.where(
                lane_wide == 0, ay_recv[which, 1, :, i : i + 1], ay_recv[which, 0, :, i : i + 1]
            )

    def fill_rims(target, which):
        for i in range(20):
            v, z = i // 4, i % 4
            target[v, z + 1, 7:8] = ax_recv[which, 0, i : i + 1]
            target[v, z + 1, 40:41] = ax_recv[which, 1, i : i + 1]
        for v in range(5):
            plane = az_recv[which, v]
            target[v, 0, 8:40] = jnp.where(gz > 0, plane, 0.0)
            target[v, 5, 8:40] = jnp.where(gz > 0, 0.0, plane)

    for load in loads[8:]:
        load.wait()
    for copy in y_copies:
        copy.wait()
    joined = recv_first[...].astype(f32) + recv_last[...].astype(f32)
    ext[...] += jnp.dot(joined.T, place_ref[...], preferred_element_type=f32)

    coarse_e = ext[0:320].reshape(40, 8, 128)
    x1_e = ext[320:640].reshape(40, 8, 128)
    y1_e = ext[640:1280].reshape(40, 16, 128)
    x2_e = ext[1280:1920].reshape(40, 16, 128)
    y2_e = ext[1920:3200].reshape(40, 32, 128)
    blank = jnp.zeros((40, 1, 128), f32)
    low = jnp.concatenate(
        [coarse_e[:, 6:8], x1_e[:, 7:8], y1_e[:, 14:16], x2_e[:, 15:16], y2_e[:, 31:32], blank], 1
    )
    high = jnp.concatenate(
        [coarse_e[:, 0:3], x1_e[:, 0:1], y1_e[:, 0:2], y2_e[:, 0:1], blank], 1
    )
    rows_low[...] = low.reshape(320, 128).astype(bf16)
    rows_high[...] = high.reshape(320, 128).astype(bf16)
    x_copies = [
        remote(2, rows_low, recv_low, x_up),
        remote(3, rows_high, recv_high, x_down),
    ]
    for copy in x_copies:
        copy.start()

    for (begin, end, width), which, at in zip(segments, (0, 0, 1, 2, 3), (0, 8, 16, 32, None)):
        product = jnp.dot(
            ext[begin:end].astype(bf16), ay_ref[which], preferred_element_type=f32
        ).reshape(40, (end - begin) // 40, 256)
        if at is None:
            mapped_y2[...] = product
        else:
            mapped[:, at : at + (end - begin) // 40] = product

    for copy in adj_copies:
        copy.wait()
    fill_rims(adj_ext, 0)
    fill_columns(adj_edge, 0)

    row_kind = lax.broadcasted_iota(jnp.int32, (320, 128), 0) % 8
    for copy in x_copies:
        copy.wait()
    for buffer, at, bounds in (
        (recv_low, 48, ((0, 3), (3, 5), (5, 6), (6, 8))),
        (recv_high, 56, ((0, 4), (4, 6), (6, 6), (6, 8))),
    ):
        received = buffer[...].astype(f32)
        total = jnp.zeros((320, 256), f32)
        for which, (begin, end) in enumerate(bounds):
            if begin < end:
                part = jnp.where((row_kind >= begin) & (row_kind < end), received, 0.0)
                total = total + jnp.dot(
                    part.astype(bf16), ay_ref[which], preferred_element_type=f32
                )
        mapped[:, at : at + 8] = total.reshape(40, 8, 256)

    def synthesize(order, cv, carry):
        for z in order:
            p = cv * 4 + z
            exact = mapped[p]
            coarse_bits = exact.astype(bf16)
            rest = (exact - coarse_bits.astype(f32)).astype(bf16)
            whole = jnp.dot(
                ax_ref[...],
                jnp.concatenate([coarse_bits, rest], axis=0),
                preferred_element_type=f32,
            )
            extra = mapped_y2[p]
            state[cv, z + 1, 0:8] = whole[0:8, 0:128]
            state[cv, z + 1, 8:40] = whole[8:40, 0:128] + extra[:, 0:128]
            state[cv, z + 1, 40:48] = whole[40:48, 0:128]
            edge[cv, z] = whole[8:40, 128:256] + extra[:, 128:256]
        return carry

    def synthesize_sides(pair, carry):
        for j in range(5):
            synthesize((z_side,), 5 * pair + j, carry)
        return carry

    lax.fori_loop(0, 2, synthesize_sides, 0)
    state_copy = remote(4, state.at[:, z_side + 1, 8:40], state_z, z_other)
    state_copy.start()
    lax.fori_loop(0, 10, functools.partial(synthesize, (gz, gz + 1, gz + 2)), 0)
    state_copy.wait()
    for cv in range(10):
        plane = state_z[cv]
        state[cv, 0, 8:40] = jnp.where(gz > 0, plane, 0.0)
        state[cv, 5, 8:40] = jnp.where(gz > 0, 0.0, plane)

    keep_bottom = jnp.where(gz > 0, 1.0, 0.0).astype(f32)

    def rate(base, source, source_edge, finish, stores=()):
        def z_faces(k, carry):
            for r in range(4):
                at = slice(8 + 8 * r, 16 + 8 * r)
                mean = [0.5 * (state[base + v, k, at] + state[base + v, k + 1, at]) for v in range(5)]
                jump = [source[v, k + 1, at] - source[v, k, at] for v in range(5)]
                terms = face(mean, jump, 2)
                factor = jnp.where(k == 0, keep_bottom, 1.0)
                for v in range(5):
                    gz_terms[v, k, 8 * r : 8 * r + 8] = terms[v] * factor
            return carry

        lax.fori_loop(0, 5, z_faces, 0)

        def plane(z, carry):
            if stores:

                @pl.when(z > 0)
                def _():
                    store(z - 1).start()

            for r in range(5):
                low_at, high_at = slice(7 + 8 * r, 15 + 8 * r), slice(8 + 8 * r, 16 + 8 * r)
                mean = [
                    0.5 * (state[base + v, z + 1, low_at] + state[base + v, z + 1, high_at])
                    for v in range(5)
                ]
                jump = [source[v, z + 1, high_at] - source[v, z + 1, low_at] for v in range(5)]
                terms = face(mean, jump, 0)
                for v in range(5):
                    gx_terms[v, 8 * r : 8 * r + 8] = terms[v]
            for r in range(4):
                at, rows = slice(8 + 8 * r, 16 + 8 * r), slice(8 * r, 8 * r + 8)
                here = [state[base + v, z + 1, at] for v in range(5)]
                rim = [edge[base + v, z, rows] for v in range(5)]
                adj = [source[v, z + 1, at] for v in range(5)]
                adj_rim = [source_edge[v, z, rows] for v in range(5)]

                def ahead(a, b):
                    return pltpu.roll(jnp.where(lane == 0, b, a), 127, 1)

                def behind(a, b):
                    return pltpu.roll(jnp.where(lane == 127, b, a), 1, 1)

                adj_up = [ahead(adj[v], adj_rim[v]) for v in range(5)]
                adj_down = [behind(adj[v], adj_rim[v]) for v in range(5)]
                up = face(
                    [0.5 * (here[v] + ahead(here[v], rim[v])) for v in range(5)],
                    [adj_up[v] - adj[v] for v in range(5)],
                    1,
                )
                down = face(
                    [0.5 * (here[v] + behind(here[v], rim[v])) for v in range(5)],
                    [adj[v] - adj_down[v] for v in range(5)],
                    1,
                )
                for v in range(5):
                    halves = (
                        up[v]
                        + down[v]
                        + gx_terms[v, rows]
                        + gx_terms[v, 8 * r + 1 : 8 * r + 9]
                        + gz_terms[v, z, rows]
                        + gz_terms[v, z + 1, rows]
                    )
                    around = (
                        adj_up[v]
                        + adj_down[v]
                        + source[v, z + 1, 7 + 8 * r : 15 + 8 * r]
                        + source[v, z + 1, 9 + 8 * r : 17 + 8 * r]
                        + source[v, z, at]
                        + source[v, z + 2, at]
                    )
                    finish(v, z, rows, at, 0.5 * halves + viscosity * (around - 6.0 * adj[v]))
            return carry

        lax.fori_loop(0, 4, plane, 0)

    def store(z):
        return pltpu.make_async_copy(out_ref.at[:, z], out_any.at[:, z], load_sem.at[11 + z])

    def finish_first(v, z, rows, at, value):
        held = adj_ext[v, z + 1, at]
        mid_ext[v, z + 1, at] = held + time_step * value
        out_ref[v, z, rows] = held + 0.5 * time_step * value

    def finish_second(v, z, rows, at, value):
        out_ref[v, z, rows] += 0.5 * time_step * value

    rate(0, adj_ext, adj_edge, finish_first)
    mid_copies = rim_copies(mid_ext.at[:, z_side + 1, 8:40], 1)
    pack_columns(mid_ext, 1)
    for copy in mid_copies[2:4]:
        copy.start()
    pack_rows(mid_ext, 1)
    for copy in mid_copies[0:2] + mid_copies[4:5]:
        copy.start()
    for copy in mid_copies[0:2] + mid_copies[4:5]:
        copy.wait()
    fill_rims(mid_ext, 1)
    for copy in mid_copies[2:4]:
        copy.wait()
    fill_columns(mid_edge, 1)
    rate(5, mid_ext, mid_edge, finish_second, stores=(0, 1, 2, 3))
    store(3).start()
    for z in range(4):
        store(z).wait()


def shards(coarse, detail_x1, detail_y1, detail_x2, detail_y2, significance, adjoint):
    anywhere = pl.BlockSpec(memory_space=pl.ANY)
    return pl.pallas_call(
        kernel,
        out_shape=jax.ShapeDtypeStruct(adjoint.shape, f32),
        in_specs=[anywhere] * 11,
        out_specs=anywhere,
        scratch_shapes=[
            pltpu.VMEM((320, 32), bf16),
            pltpu.VMEM((320, 32), bf16),
            pltpu.VMEM((640, 32), bf16),
            pltpu.VMEM((640, 64), bf16),
            pltpu.VMEM((1280, 64), bf16),
            pltpu.VMEM((2, 4, 4, 4), jnp.int32),
            pltpu.VMEM((5, 4, 32, 128), f32),
            pltpu.VMEM((4, 128, 256), bf16),
            pltpu.VMEM((48, 128), bf16),
            pltpu.VMEM((2, 16, 64), bf16),
            pltpu.VMEM((8, 128), f32),
            pltpu.VMEM((5, 4, 32, 128), f32),
            pltpu.SemaphoreType.DMA((15,)),
            pltpu.VMEM((2, 4, 8, 64), f32),
            pltpu.VMEM((2, 4, 16, 64), f32),
            pltpu.VMEM((2, 4, 32, 64), f32),
            pltpu.VMEM((3200, 128), f32),
            pltpu.VMEM((8, 3200), bf16),
            pltpu.VMEM((8, 3200), bf16),
            pltpu.VMEM((8, 3200), bf16),
            pltpu.VMEM((8, 3200), bf16),
            pltpu.VMEM((320, 128), bf16),
            pltpu.VMEM((320, 128), bf16),
            pltpu.VMEM((320, 128), bf16),
            pltpu.VMEM((320, 128), bf16),
            pltpu.VMEM((40, 64, 256), f32),
            pltpu.VMEM((40, 32, 256), f32),
            pltpu.VMEM((10, 6, 48, 128), f32),
            pltpu.VMEM((10, 4, 32, 128), f32),
            pltpu.VMEM((10, 32, 128), f32),
            pltpu.VMEM((5, 6, 48, 128), f32),
            pltpu.VMEM((5, 4, 32, 128), f32),
            pltpu.VMEM((5, 6, 48, 128), f32),
            pltpu.VMEM((5, 4, 32, 128), f32),
            pltpu.VMEM((2, 2, 24, 128), f32),
            pltpu.VMEM((2, 2, 24, 128), f32),
            pltpu.VMEM((2, 2, 32, 128), f32),
            pltpu.VMEM((2, 2, 32, 128), f32),
            pltpu.VMEM((8, 128), f32),
            pltpu.VMEM((2, 5, 32, 128), f32),
            pltpu.VMEM((5, 40, 128), f32),
            pltpu.VMEM((5, 5, 32, 128), f32),
            pltpu.SemaphoreType.DMA((15,)),
            pltpu.SemaphoreType.DMA((15,)),
        ],
        compiler_params=pltpu.CompilerParams(collective_id=0, has_side_effects=True),
    )(
        coarse.reshape(320, 32),
        detail_x1.reshape(320, 32),
        detail_y1.reshape(640, 32),
        detail_x2.reshape(640, 64),
        detail_y2.reshape(1280, 64),
        significance,
        adjoint,
        jnp.asarray(y_matrices()),
        jnp.asarray(x_matrix()),
        jnp.asarray(pick_matrices()),
        jnp.asarray(place_matrix()),
    )


def solution(mesh):
    return jax.shard_map(
        shards,
        mesh=mesh,
        in_specs=(
            P(None, None, "gz", "gx", "gy"),
            P(None, None, "gz", "gx", "gy"),
            P(None, None, "gz", "gx", "gy"),
            P(None, None, "gz", "gx", "gy"),
            P(None, None, "gz", "gx", "gy"),
            P(None, "gz", "gx", "gy"),
            P(None, "gz", "gx", "gy"),
        ),
        out_specs=P(None, "gz", "gx", "gy"),
        check_vma=False,
    )
```
